256 devices in a mesh: dp: 32 (over x, y, core), expert: 8 (over z).
Axes of the slice: x: 4, y: 4, z: 8, core: 2. Of those that a mesh axis runs over, the one named last changes fastest.
Arguments:
- expert_master: float32 [8, 7168, 2048], P('expert', 'dp'), may hold values from -6 to 6
- expert_first: bfloat16 [8, 7168, 2048], P('expert', 'dp'), may hold values from -0.29882812 to 0.29882812
- expert_second: bfloat16 [8, 7168, 2048], P('expert', 'dp'), may hold values from 9.9658966e-05 to 0.0099487305
- expert_grad: bfloat16 [8, 7168, 2048], P('expert', 'dp'), may hold values from -0.29882812 to 0.29882812
- latent_master: float32 [7168, 1536], P(('dp', 'expert')), may hold values from -6 to 6
- latent_first: bfloat16 [7168, 1536], P(('dp', 'expert')), may hold values from -0.29882812 to 0.29882812
- latent_second: bfloat16 [7168, 1536], P(('dp', 'expert')), may hold values from 9.9658966e-05 to 0.0099487305
- latent_grad: bfloat16 [7168, 1536], P(('dp', 'expert')), may hold values from -0.29882812 to 0.29882812
- step_count: int32 [1], replicated, may hold values from 1 to 11
- column_owner: int32 [16], replicated, may hold values from 0 to 15, each once
Outputs:
- expert_master_new: float32 [8, 7168, 2048], P('expert', 'dp')
- expert_first_new: bfloat16 [8, 7168, 2048], P('expert', 'dp')
- expert_second_new: bfloat16 [8, 7168, 2048], P('expert', 'dp')
- expert_served: bfloat16 [8, 114688, 128], P('expert', 'dp')
- expert_scales: float32 [8, 896], P('expert', 'dp')
- latent_master_new: float32 [7168, 1536], P(('dp', 'expert'))
- latent_first_new: bfloat16 [7168, 1536], P(('dp', 'expert'))
- latent_second_new: bfloat16 [7168, 1536], P(('dp', 'expert'))
- latent_served: bfloat16 [7168, 1536], P('dp')
- latent_scales: float32 [56, 12], replicated
The draws below stay inside these ranges and needn't reach their ends.
Inputs may be any that keep to these rules, and one draw needn't show every extreme that they name: column_owner names each serving position of the 16 column blocks exactly once.
All inputs are finite; a program needn't handle non-finite values. Where the reference program divides by a largest or mean magnitude, that divisor is 1e-20 or more.
Results may differ from the reference program's by a relative error of at most 0.0017.
Values may be sent and summed in bfloat16 or wider, within the bound.
A program may use at most 64 MiB of HBM per device.

```python
import math
import jax
import jax.numpy as jnp
from jax import lax

D = 7168
F = 2048
FM = 1536
TILE = 128
EXPERTS = 8


def shard_levels(stream_key, shape, shards, smallest, high):
    def one(axis_at, blocks):
        heights = jax.random.uniform(jax.random.fold_in(jax.random.fold_in(stream_key, 6), axis_at), (blocks,), jnp.float32, smallest / len(shards), high / len(shards))
        return jnp.repeat(jnp.exp(heights), shape[axis_at] // blocks).reshape((-1,) + (1,) * (len(shape) - axis_at - 1))

    factor_of = one(*shards[0])
    for cut in shards[1:]:
        factor_of = factor_of * one(*cut)
    return factor_of


def noise(own_key, extent, width, bound, split=(), kind=jnp.bfloat16):
    loudness = shard_levels(own_key, extent, split, -0.22, 0.18) if split else 1.0
    entries = jax.random.normal(own_key, extent, jnp.float32) * width * loudness
    return jnp.minimum(jnp.maximum(entries, -bound), bound).astype(kind)


def setup_inputs(seed: int = 0) -> dict:
    key_list = jax.random.split(jax.random.key(seed), 11)
    return {
        "expert_master": noise(key_list[0], (EXPERTS, D, F), 1.0, 6.0, ((0, 8), (1, 32)), jnp.float32),
        "expert_first": noise(key_list[1], (EXPERTS, D, F), 0.05, 0.29882812, ((0, 8), (1, 32))),
        "expert_second": jnp.clip(jnp.exp(math.log(0.0099487305) - 4.603446 * jax.random.uniform(key_list[2], (EXPERTS, D, F), jnp.float32) ** shard_levels(key_list[2], (EXPERTS, D, F), ((0, 8), (1, 32)), -0.2, 0.2)), 9.965896606445312e-05, 0.0099487305).astype(jnp.bfloat16),
        "expert_grad": noise(key_list[3], (EXPERTS, D, F), 0.05, 0.29882812, ((0, 8), (1, 32))),
        "latent_master": noise(key_list[4], (D, FM), 1.0, 6.0, ((0, 256),), jnp.float32),
        "latent_first": noise(key_list[5], (D, FM), 0.05, 0.29882812, ((0, 256),)),
        "latent_second": jnp.clip(jnp.exp(math.log(0.0099487305) - 4.603446 * jax.random.uniform(key_list[6], (D, FM), jnp.float32) ** shard_levels(key_list[6], (D, FM), ((0, 256),), -0.2, 0.2)), 9.965896606445312e-05, 0.0099487305).astype(jnp.bfloat16),
        "latent_grad": noise(key_list[7], (D, FM), 0.05, 0.29882812, ((0, 256),)),
        "step_count": jax.random.randint(key_list[8], (1,), 1, 12).astype(jnp.int32),
        "column_owner": jax.random.permutation(key_list[9], F // TILE).astype(jnp.int32),
    }


BETA_ONE = 0.9
BETA_TWO = 0.95
LEARN_RATE = 0.2
DECAY_RATE = 0.1
ADAM_EPS = 1e-08
SCALE_EPS = 1e-06

def adamw_step(master, moment_one, moment_two, gradient, step_count):
    grad_value = gradient.astype(jnp.float32)
    first_new = BETA_ONE * moment_one.astype(jnp.float32) + (1.0 - BETA_ONE) * grad_value
    second_new = BETA_TWO * moment_two.astype(jnp.float32) + (1.0 - BETA_TWO) * grad_value * grad_value
    step_value = step_count[0].astype(jnp.float32)
    corr_one = 1.0 - jnp.power(jnp.float32(BETA_ONE), step_value)
    corr_two = 1.0 - jnp.power(jnp.float32(BETA_TWO), step_value)
    update = first_new / corr_one / (jnp.sqrt(second_new / corr_two) + ADAM_EPS)
    master_new = master - LEARN_RATE * (update + DECAY_RATE * master)
    return (master_new, first_new.astype(jnp.bfloat16), second_new.astype(jnp.bfloat16))

def quantize_full(weights):
    row_count, col_count = weights.shape
    blocks = weights.reshape(row_count // TILE, TILE, col_count // TILE, TILE)
    block_max = lax.optimization_barrier(jnp.max(jnp.abs(blocks), axis=(1, 3)))
    scaled = blocks / (block_max[:, None, :, None] + SCALE_EPS)
    return (scaled.reshape(row_count, col_count).astype(jnp.bfloat16), block_max)

def reference(expert_master, expert_first, expert_second, expert_grad, latent_master, latent_first, latent_second, latent_grad, step_count, column_owner):

    def per_expert(items):
        master, moment_one, moment_two, gradient = items
        master_new, first_new, second_new = adamw_step(master, moment_one, moment_two, gradient, step_count)
        scaled, block_max = quantize_full(master_new)
        return (master_new, first_new, second_new, scaled, block_max)
    master_out, first_out, second_out, scaled_all, maxima_all = lax.map(per_expert, (expert_master, expert_first, expert_second, expert_grad))
    block_count = F // TILE
    positions = jnp.arange(block_count, dtype=jnp.int32)
    inverse = lax.optimization_barrier(jnp.sum(positions[:, None] * (column_owner[:, None] == positions[None, :]).astype(jnp.int32), axis=0)).astype(jnp.int32)
    served = jnp.take(scaled_all.reshape(EXPERTS, D, block_count, TILE), inverse, axis=2)
    served = jnp.transpose(served, (0, 2, 1, 3)).reshape(EXPERTS, block_count * D, TILE)
    scales = jnp.take(maxima_all, inverse, axis=2)
    scales = jnp.transpose(scales, (0, 2, 1)).reshape(EXPERTS, block_count * (D // TILE))
    latent_new, latent_one, latent_two = adamw_step(latent_master, latent_first, latent_second, latent_grad, step_count)
    latent_out, latent_scales = quantize_full(latent_new)
    return (master_out, first_out, second_out, served, scales, latent_new, latent_one, latent_two, latent_out, latent_scales)
```

```python
import jax
import jax.numpy as jnp
from jax import lax
from jax.experimental import pallas as pl
from jax.experimental.pallas import tpu as pltpu
from jax.sharding import Mesh
from jax.sharding import PartitionSpec as P

MESH = pl.DeviceIdType.MESH
TILE = 128
DP = ("dp_0", "dp_1", "dp_2")
DP_EXPERT = ("dp_0", "dp_1", "dp_2", "expert")

BETA_ONE = 0.9
BETA_TWO = 0.95
LEARN_RATE = 0.2
DECAY_RATE = 0.1
ADAM_EPS = 1e-08
SCALE_EPS = 1e-06

ROWS = 224
COLS = 2048
BLOCKS = COLS // TILE
SUB = 32
LROWS = 28
LCOLS = 1536
LBLOCKS = LCOLS // TILE
HALF = LCOLS // 2
LANE0 = 32
LINKS = 17

f32 = jnp.float32
bf16 = jnp.bfloat16


def iota2(shape, dim):
    return lax.broadcasted_iota(jnp.int32, shape, dim)


def adamw(master, first, second, grad, num_scale, den_scale):
    g = grad.astype(f32)
    first_new = BETA_ONE * first.astype(f32) + (1.0 - BETA_ONE) * g
    second_new = BETA_TWO * second.astype(f32) + (1.0 - BETA_TWO) * g * g
    update = (first_new * num_scale) / (jnp.sqrt(second_new * den_scale) + ADAM_EPS)
    master_new = (1.0 - LEARN_RATE * DECAY_RATE) * master - update
    return master_new, first_new.astype(bf16), second_new.astype(bf16)


def fold_rows(value):
    rows = value.shape[0]
    out = value[0:8]
    for r in range(8, rows, 8):
        out = jnp.maximum(out, value[r : r + 8])
    return out


def lanes_of(rows_value, first_lane):
    spread = jnp.broadcast_to(rows_value, (16, TILE))
    hit = iota2((16, TILE), 1) == iota2((16, TILE), 0) + first_lane
    return jnp.max(jnp.where(hit, spread, 0.0), axis=0, keepdims=True)


def blocks_of(row, first_lane):
    spread = jnp.broadcast_to(row, (16, TILE))
    hit = iota2((16, TILE), 1) == iota2((16, TILE), 0) + first_lane
    return jnp.max(jnp.where(hit, spread, 0.0), axis=1, keepdims=True)


def step_kernel(
    owner,
    step_count,
    w_hbm,
    m_hbm,
    v_hbm,
    g_hbm,
    lw_hbm,
    lm_hbm,
    lv_hbm,
    lg_hbm,
    w_out,
    m_out,
    v_out,
    served,
    rows_all,
    lw_out,
    lm_out,
    lv_out,
    lat,
    w_in,
    m_in,
    v_in,
    g_in,
    lw_in,
    lm_in,
    lv_in,
    lg_in,
    w_blocks,
    send,
    own_fold,
    next_fold,
    prev_fold,
    own_scale,
    own_recip,
    next_recip,
    prev_recip,
    next_scale,
    lfold_a,
    lfold_b,
    lrecip_a,
    lrecip_b,
    lrow_out,
    lrow_in,
    edge_out,
    edge_in,
    rows_out,
    inverse,
    in_sem,
    bulk_send,
    bulk_recv,
    self_sem,
    lrow_send,
    lrow_recv,
    edge_send,
    edge_recv,
    rows_send,
    rows_recv,
    ring_send,
    ring_recv,
):
    x = lax.axis_index("dp_0")
    y = lax.axis_index("dp_1")
    c = lax.axis_index("dp_2")
    z = lax.axis_index("expert")
    dp = (x * 4 + y) * 2 + c
    inner = lax.rem(y, 2) * 2 + c
    quad = lax.div(y, 2) * 2
    half = lax.div(x, 2)
    slot = lax.rem(dp, 16)
    is_self = c == half

    def dp_device(target, target_z):
        return (lax.div(target, 8), lax.rem(lax.div(target, 2), 4), lax.rem(target, 2), target_z)

    def quad_device(place, target_z):
        return (x, quad + lax.div(place, 2), lax.rem(place, 2), target_z)

    def up(value, n):
        return lax.rem(value, n)

    inner_next = up(inner + 1, 4)
    inner_prev = up(inner + 3, 4)

    loads = []

    def load(src, dst):
        copy = pltpu.make_async_copy(src, dst, in_sem.at[len(loads)])
        copy.start()
        loads.append(copy)

    for src, dst in ((lw_hbm, lw_in), (lm_hbm, lm_in), (lv_hbm, lv_in), (lg_hbm, lg_in)):
        load(src, dst)
    slabs = [pl.multiple_of(up(inner + j, 7) * SUB, SUB) for j in range(4, 7)]
    local = pl.multiple_of(inner * SUB, SUB)
    pairs = ((w_hbm, w_in), (m_hbm, m_in), (v_hbm, v_in), (g_hbm, g_in))
    for src, dst in pairs:
        for s in slabs:
            load(src.at[pl.ds(s, SUB), :], dst.at[pl.ds(s, SUB), :])
    for src, dst in pairs:
        load(src.at[pl.ds(local, TILE), :], dst.at[pl.ds(local, TILE), :])

    barrier = pltpu.get_barrier_semaphore()

    def greet(device):
        pl.semaphore_signal(barrier, inc=1, device_id=device, device_id_type=MESH)

    @pl.loop(1, 8)
    def _(d):
        greet((x, y, c, up(z + d, 8)))

    @pl.loop(1, 6)
    def _(d):
        greet(quad_device(inner_next, up(z + d, 8)))

    @pl.loop(3, 8)
    def _(d):
        greet(quad_device(inner_prev, up(z + d, 8)))

    @pl.loop(1, 32)
    def _(d):
        greet(dp_device(up(dp + d, 32), z))

    @pl.loop(0, 16)
    def _(k):
        p = up(x + lax.div(k, 4), 4) * 4 + up(y + lax.rem(k, 4), 4)
        total = jnp.int32(0)
        for b in range(BLOCKS):
            total = jnp.maximum(total, jnp.where(owner[b] == p, b, 0))
        inverse[k] = total

    steps = jnp.full((8, TILE), step_count[0], jnp.int32).astype(f32)
    num_scale = (LEARN_RATE / (1.0 - jnp.power(jnp.full((8, TILE), BETA_ONE, f32), steps)))[0:1]
    den_scale = (1.0 / (1.0 - jnp.power(jnp.full((8, TILE), BETA_TWO, f32), steps)))[0:1]

    for copy in loads[:4]:
        copy.wait()
    lat_place = (inner * 8 + z) * LROWS
    lat_block = lax.div(lat_place, TILE)
    lat_edge = TILE - lax.rem(lat_place, TILE)
    lat_rows = iota2((LROWS, TILE), 0)

    for b in range(LBLOCKS):
        cols = pl.ds(b * TILE, TILE)
        w1, m1, v1 = adamw(
            lw_in[:, cols], lm_in[:, cols], lv_in[:, cols], lg_in[:, cols], num_scale, den_scale
        )
        lw_out[:, cols] = w1
        lm_out[:, cols] = m1
        lv_out[:, cols] = v1
        size = jnp.abs(w1)
        lfold_a[b : b + 1, :] = jnp.max(
            jnp.where(lat_rows < lat_edge, size, 0.0), axis=0, keepdims=True
        )
        lfold_b[b : b + 1, :] = jnp.max(
            jnp.where(lat_rows >= lat_edge, size, 0.0), axis=0, keepdims=True
        )
    real = iota2((16, 1), 0) < LBLOCKS
    first_lane = LANE0 + lat_block * LBLOCKS
    max_a = jnp.where(real, jnp.max(lfold_a[...], axis=1, keepdims=True), 0.0)
    max_b = jnp.where(real, jnp.max(lfold_b[...], axis=1, keepdims=True), 0.0)
    lrow = jnp.maximum(lanes_of(max_a, first_lane), lanes_of(max_b, first_lane + LBLOCKS))
    lrow_out[0] = lrow

    for copy in loads[4:16]:
        copy.wait()

    @pl.loop(0, BLOCKS)
    def _(b):
        cols = pl.ds(pl.multiple_of(b * TILE, TILE), TILE)
        after = jnp.zeros((8, TILE), f32)
        before = jnp.zeros((8, TILE), f32)
        for j, s in zip(range(4, 7), slabs):
            rows = pl.ds(s, SUB)
            w1, m1, v1 = adamw(
                w_in[rows, cols], m_in[rows, cols], v_in[rows, cols], g_in[rows, cols],
                num_scale, den_scale,
            )
            w_out[rows, cols] = w1
            w_blocks[b, rows, :] = w1
            m_out[rows, cols] = m1
            v_out[rows, cols] = v1
            size = fold_rows(jnp.abs(w1))
            is_after = inner + j < 7
            after = jnp.maximum(after, jnp.where(is_after, size, 0.0))
            before = jnp.maximum(before, jnp.where(is_after, 0.0, size))
        next_fold[b] = after
        prev_fold[b] = before

    def widest(fold):
        return jnp.max(jnp.max(fold[...], axis=1), axis=1, keepdims=True)

    edge_out[0] = lanes_of(widest(next_fold), 0)
    edge_out[1] = lanes_of(widest(prev_fold), 0)

    pl.semaphore_wait(barrier, LINKS + 31)

    def edge_copy(n, place):
        return pltpu.make_async_remote_copy(
            src_ref=edge_out.at[n],
            dst_ref=edge_in.at[n],
            send_sem=edge_send.at[n],
            recv_sem=edge_recv.at[n],
            device_id=quad_device(place, z),
            device_id_type=MESH,
        )

    edges = [edge_copy(0, inner_next), edge_copy(1, inner_prev)]
    for copy in edges:
        copy.start()

    def lrow_copy(n, device):
        return pltpu.make_async_remote_copy(
            src_ref=lrow_out.at[0],
            dst_ref=lrow_in.at[n],
            send_sem=lrow_send,
            recv_sem=lrow_recv,
            device_id=device,
            device_id_type=MESH,
        )

    @pl.loop(1, 8)
    def _(d):
        lrow_copy(d - 1, (x, y, c, up(z + d, 8))).start()

    @pl.loop(1, 6)
    def _(d):
        lrow_copy(d + 6, quad_device(inner_next, up(z + d, 8))).start()

    @pl.loop(3, 8)
    def _(d):
        lrow_copy(d + 9, quad_device(inner_prev, up(z + d, 8))).start()

    for copy in loads[16:]:
        copy.wait()
    own = pl.ds(local, TILE)

    @pl.loop(0, BLOCKS)
    def _(b):
        cols = pl.ds(pl.multiple_of(b * TILE, TILE), TILE)
        w1, m1, v1 = adamw(
            w_in[own, cols], m_in[own, cols], v_in[own, cols], g_in[own, cols], num_scale, den_scale
        )
        w_out[own, cols] = w1
        w_blocks[b, own, :] = w1
        m_out[own, cols] = m1
        v_out[own, cols] = v1
        own_fold[b] = fold_rows(jnp.abs(w1))

    def spread(scale):
        return jnp.broadcast_to(scale, (16, TILE))

    def recip(scale):
        return spread(1.0 / (scale + SCALE_EPS))

    def put(ref, value):
        for b in range(BLOCKS):
            ref[b] = value[b : b + 1]

    own_max = widest(own_fold)
    put(own_scale, spread(own_max))
    put(own_recip, recip(own_max))

    def target(k):
        return (up(x + lax.div(k, 4), 4), up(y + lax.rem(k, 4), 4), half, z)

    def bulk(k, rows, start):
        src = send.at[k, pl.ds(rows, start[1]), :]
        dst = served.at[slot, pl.ds(rows, start[1]), :]
        return src, dst

    def bulk_start(k, rows, count):
        src = send.at[k, pl.ds(rows, count), :]
        dst = served.at[slot, pl.ds(rows, count), :]
        stays = jnp.logical_and(is_self, k == 0)

        @pl.when(stays)
        def _():
            pltpu.make_async_copy(src, dst, self_sem).start()

        @pl.when(jnp.logical_not(stays))
        def _():
            pltpu.make_async_remote_copy(
                src_ref=src,
                dst_ref=dst,
                send_sem=bulk_send,
                recv_sem=bulk_recv,
                device_id=target(k),
                device_id_type=MESH,
            ).start()

    @pl.loop(0, 16)
    def _(k):
        b = inverse[k]
        send[k, own, :] = (w_blocks[b, own, :] * own_recip[b]).astype(bf16)

    @pl.loop(0, 16)
    def _(k):
        bulk_start(k, local, TILE)

    for copy in edges:
        copy.wait_recv()
    prev_max = blocks_of(jnp.maximum(edge_out[1], edge_in[0]), 0)
    next_max = blocks_of(jnp.maximum(edge_out[0], edge_in[1]), 0)
    put(prev_recip, recip(prev_max))
    put(next_recip, recip(next_max))
    put(next_scale, spread(next_max))

    @pl.loop(0, 16)
    def _(k):
        b = inverse[k]
        after = next_recip[b]
        before = prev_recip[b]
        for j, s in zip(range(4, 7), slabs):
            rows = pl.ds(s, SUB)
            scale = jnp.where(inner + j < 7, after, before)
            send[k, rows, :] = (w_blocks[b, rows, :] * scale).astype(bf16)

    pltpu.make_async_copy(lrow_in, lrow_in, lrow_recv).wait()
    lmax = jnp.maximum(lrow, jnp.max(lrow_in[...], axis=0))
    lrecip_a[...] = recip(blocks_of(lmax, first_lane))
    lrecip_b[...] = recip(blocks_of(lmax, first_lane + LBLOCKS))

    for b in range(LBLOCKS):
        cols = pl.ds(b * TILE, TILE)
        scale = jnp.where(lat_rows < lat_edge, lrecip_a[b : b + 1, :], lrecip_b[b : b + 1, :])
        lat[z, :, cols] = (lw_out[:, cols] * scale).astype(bf16)

    lane = iota2((1, TILE), 1)
    scale_lane = 7 * lax.div(slot, 4) + 2 * inner
    lat_lanes = jnp.where(lane >= LANE0, lmax, 0.0)

    def message(k):
        b = inverse[k]
        value = jnp.where(lane == scale_lane, own_scale[b], lat_lanes)
        both = jnp.logical_and(lane == scale_lane + 1, inner < 3)
        return jnp.where(both, next_scale[b], value)

    @pl.loop(0, 16)
    def _(k):
        rows_out[k] = message(k)

    def ring_copy(way, hop, part):
        origin = up(z + 8 - hop, 8) if way == 0 else up(z + hop, 8)
        peer = up(z + 1, 8) if way == 0 else up(z + 7, 8)
        view = lat.at[origin, :, pl.ds(part * HALF, HALF)]
        n = (way * 4 + hop) * 2 + part
        return pltpu.make_async_remote_copy(
            src_ref=view,
            dst_ref=view,
            send_sem=ring_send.at[n],
            recv_sem=ring_recv.at[n],
            device_id=(x, y, c, peer),
            device_id_type=MESH,
        )

    def arrived(way, hop, part):
        origin = up(z + 7 - hop, 8) if way == 0 else up(z + 1 + hop, 8)
        view = lat.at[origin, :, pl.ds(part * HALF, HALF)]
        n = (way * 4 + hop) * 2 + part
        pltpu.make_async_copy(view, view, ring_recv.at[n]).wait()

    hops = [
        (way, hop, part)
        for hop in range(4)
        for part in range(2)
        for way in range(2)
        if hop < 3 or part == way
    ]
    sent = []
    for way, hop, part in hops:
        if hop == 0:
            copy = ring_copy(way, hop, part)
            copy.start()
            sent.append(copy)

    def rows_copy(k, core):
        return pltpu.make_async_remote_copy(
            src_ref=rows_out.at[k],
            dst_ref=rows_all.at[dp],
            send_sem=rows_send,
            recv_sem=rows_recv,
            device_id=(up(x + lax.div(k, 4), 4), up(y + lax.rem(k, 4), 4), core, z),
            device_id_type=MESH,
        )

    rows_all[dp] = rows_out[0]
    rows_copy(0, 1 - c).start()

    @pl.loop(1, 16)
    def _(k):
        rows_copy(k, 0).start()
        rows_copy(k, 1).start()

    for j, s in zip(range(4, 7), slabs):

        @pl.loop(0, 16)
        def _(k):
            bulk_start(k, s, SUB)

    for way, hop, part in hops:
        arrived(way, hop, part)
        if (way, hop + 1, part) in hops:
            copy = ring_copy(way, hop + 1, part)
            copy.start()
            sent.append(copy)

    for copy in sent:
        copy.wait_send()
    for copy in edges:
        copy.wait_send()
    pltpu.make_async_copy(lrow_in, lrow_in, lrow_send).wait()
    few = rows_all.at[pl.ds(0, 31)]
    pltpu.make_async_copy(few, few, rows_send).wait()
    pltpu.make_async_copy(few, few, rows_recv).wait()

    @pl.when(is_self)
    def _():
        one = served.at[0]
        rest = served.at[pl.ds(0, 15)]
        pltpu.make_async_copy(one, one, self_sem).wait()
        pltpu.make_async_copy(rest, rest, bulk_send).wait()
        pltpu.make_async_copy(rest, rest, bulk_recv).wait()

    @pl.when(jnp.logical_not(is_self))
    def _():
        pltpu.make_async_copy(served, served, bulk_send).wait()
        pltpu.make_async_copy(served, served, bulk_recv).wait()


def store_kernel(
    w_in,
    m_in,
    v_in,
    served_in,
    rows_in,
    lw_in,
    lm_in,
    lv_in,
    lat_in,
    w_hbm,
    m_hbm,
    v_hbm,
    served_hbm,
    scales_hbm,
    lw_hbm,
    lm_hbm,
    lv_hbm,
    lserved_hbm,
    lscales_hbm,
    lserved,
    scales,
    lscales,
    lscales_tall,
    sem,
):
    copies = []

    def store(src, dst):
        copy = pltpu.make_async_copy(src, dst, sem.at[len(copies)])
        copy.start()
        copies.append(copy)

    for src, dst in (
        (w_in, w_hbm),
        (m_in, m_hbm),
        (v_in, v_hbm),
        (served_in, served_hbm),
        (lw_in, lw_hbm),
        (lm_in, lm_hbm),
        (lv_in, lv_hbm),
    ):
        store(src, dst)
    for o in range(8):
        lserved[o * LROWS : (o + 1) * LROWS, :] = lat_in[o]
    store(lserved, lserved_hbm)
    c = lax.axis_index("dp_2")
    mine = jnp.max(rows_in[pl.ds(c * 16, 16)], axis=0)
    scales[...] = mine[:, 0:28]
    for g in range(8):
        group = jnp.max(rows_in[4 * g : 4 * g + 4], axis=0)
        for r in range(7):
            lane = LANE0 + r * LBLOCKS
            lscales_tall[7 * g + r : 7 * g + r + 1, 0:LBLOCKS] = group[:, lane : lane + LBLOCKS]
    lscales[...] = lscales_tall[...].T[0:LBLOCKS, 0:56]
    store(scales, scales_hbm)
    store(lscales, lscales_hbm)
    for copy in copies:
        copy.wait()


def body(
    expert_master,
    expert_first,
    expert_second,
    expert_grad,
    latent_master,
    latent_first,
    latent_second,
    latent_grad,
    step_count,
    column_owner,
):
    smem = pl.BlockSpec(memory_space=pltpu.SMEM)
    hbm = pl.BlockSpec(memory_space=pltpu.HBM)
    vmem = pl.BlockSpec(memory_space=pltpu.VMEM)
    dma = pltpu.SemaphoreType.DMA
    row = (1, TILE)
    made = pl.pallas_call(
        step_kernel,
        out_shape=(
            pltpu.VMEM((ROWS, COLS), f32),
            pltpu.VMEM((ROWS, COLS), bf16),
            pltpu.VMEM((ROWS, COLS), bf16),
            pltpu.VMEM((16, ROWS, TILE), bf16),
            pltpu.VMEM((32, *row), f32),
            pltpu.VMEM((LROWS, LCOLS), f32),
            pltpu.VMEM((LROWS, LCOLS), bf16),
            pltpu.VMEM((LROWS, LCOLS), bf16),
            pltpu.VMEM((8, LROWS, LCOLS), bf16),
        ),
        in_specs=[smem, smem] + [hbm] * 8,
        out_specs=(vmem,) * 9,
        scratch_shapes=[
            pltpu.VMEM((ROWS, COLS), f32),
            pltpu.VMEM((ROWS, COLS), bf16),
            pltpu.VMEM((ROWS, COLS), bf16),
            pltpu.VMEM((ROWS, COLS), bf16),
            pltpu.VMEM((LROWS, LCOLS), f32),
            pltpu.VMEM((LROWS, LCOLS), bf16),
            pltpu.VMEM((LROWS, LCOLS), bf16),
            pltpu.VMEM((LROWS, LCOLS), bf16),
            pltpu.VMEM((16, ROWS, TILE), f32),
            pltpu.VMEM((16, ROWS, TILE), bf16),
            pltpu.VMEM((16, 8, TILE), f32),
            pltpu.VMEM((16, 8, TILE), f32),
            pltpu.VMEM((16, 8, TILE), f32),
            pltpu.VMEM((16, *row), f32),
            pltpu.VMEM((16, *row), f32),
            pltpu.VMEM((16, *row), f32),
            pltpu.VMEM((16, *row), f32),
            pltpu.VMEM((16, *row), f32),
            pltpu.VMEM((16, TILE), f32),
            pltpu.VMEM((16, TILE), f32),
            pltpu.VMEM((16, TILE), f32),
            pltpu.VMEM((16, TILE), f32),
            pltpu.VMEM((1, *row), f32),
            pltpu.VMEM((LINKS, *row), f32),
            pltpu.VMEM((2, *row), f32),
            pltpu.VMEM((2, *row), f32),
            pltpu.VMEM((16, *row), f32),
            pltpu.SMEM((16,), jnp.int32),
            dma((20,)),
            dma,
            dma,
            dma,
            dma,
            dma,
            dma((2,)),
            dma((2,)),
            dma,
            dma,
            dma((16,)),
            dma((16,)),
        ],
        compiler_params=pltpu.CompilerParams(
            collective_id=0, has_side_effects=True, vmem_limit_bytes=24 << 20
        ),
        name="step",
    )(
        column_owner,
        step_count,
        *(
            pltpu.with_memory_space_constraint(value, pltpu.HBM)
            for value in (
                expert_master[0],
                expert_first[0],
                expert_second[0],
                expert_grad[0],
                latent_master,
                latent_first,
                latent_second,
                latent_grad,
            )
        ),
    )
    out = pl.pallas_call(
        store_kernel,
        out_shape=(
            jax.ShapeDtypeStruct((ROWS, COLS), f32),
            jax.ShapeDtypeStruct((ROWS, COLS), bf16),
            jax.ShapeDtypeStruct((ROWS, COLS), bf16),
            jax.ShapeDtypeStruct((16, ROWS, TILE), bf16),
            jax.ShapeDtypeStruct((1, 28), f32),
            jax.ShapeDtypeStruct((LROWS, LCOLS), f32),
            jax.ShapeDtypeStruct((LROWS, LCOLS), bf16),
            jax.ShapeDtypeStruct((LROWS, LCOLS), bf16),
            jax.ShapeDtypeStruct((ROWS, LCOLS), bf16),
            jax.ShapeDtypeStruct((LBLOCKS, 56), f32),
        ),
        in_specs=[vmem] * 9,
        out_specs=(hbm,) * 10,
        scratch_shapes=[
            pltpu.VMEM((ROWS, LCOLS), bf16),
            pltpu.VMEM((1, 28), f32),
            pltpu.VMEM((LBLOCKS, 56), f32),
            pltpu.VMEM((TILE, TILE), f32),
            dma((10,)),
        ],
        compiler_params=pltpu.CompilerParams(vmem_limit_bytes=8 << 20),
        name="store",
    )(*made)
    master, first, second, served, scales, lmaster, lfirst, lsecond, lserved, lscales = out
    return (
        master[None],
        first[None],
        second[None],
        served.reshape(1, 16 * ROWS, TILE),
        scales,
        lmaster,
        lfirst,
        lsecond,
        lserved,
        lscales.T,
    )


def solution(mesh):
    torus = Mesh(
        mesh.devices.reshape(4, 4, 2, mesh.shape["expert"]), ("dp_0", "dp_1", "dp_2", "expert")
    )
    expert = P("expert", DP, None)
    latent = P(DP_EXPERT, None)
    return jax.shard_map(
        body,
        mesh=torus,
        in_specs=(expert,) * 4 + (latent,) * 4 + (P(), P()),
        out_specs=(
            expert,
            expert,
            expert,
            expert,
            P("expert", DP),
            latent,
            latent,
            latent,
            P(DP, None),
            P(),
        ),
        check_vma=False,
    )
```

```python
import jax
import jax.numpy as jnp
from jax import lax
from jax.experimental import pallas as pl
from jax.experimental.pallas import tpu as pltpu
from jax.sharding import Mesh
from jax.sharding import PartitionSpec as P

MESH = pl.DeviceIdType.MESH
TILE = 128
DP = ("dp_0", "dp_1", "dp_2")
DP_EXPERT = ("dp_0", "dp_1", "dp_2", "expert")

BETA_ONE = 0.9
BETA_TWO = 0.95
LEARN_RATE = 0.2
DECAY_RATE = 0.1
ADAM_EPS = 1e-08
SCALE_EPS = 1e-06

ROWS = 224
COLS = 2048
BLOCKS = COLS // TILE
SUB = 32
LROWS = 28
LCOLS = 1536
LBLOCKS = LCOLS // TILE
LFLAT = LROWS * LBLOCKS
PARTS = 2
PART = LFLAT // PARTS
LANE0 = 32
GROUP = 32

f32 = jnp.float32
bf16 = jnp.bfloat16


def iota2(shape, dim):
    return lax.broadcasted_iota(jnp.int32, shape, dim)


def adamw(master, first, second, grad, num_scale, den_scale):
    g = grad.astype(f32)
    first_new = BETA_ONE * first.astype(f32) + (1.0 - BETA_ONE) * g
    second_new = BETA_TWO * second.astype(f32) + (1.0 - BETA_TWO) * g * g
    update = (first_new * num_scale) / (jnp.sqrt(second_new * den_scale) + ADAM_EPS)
    master_new = (1.0 - LEARN_RATE * DECAY_RATE) * master - update
    return master_new, first_new.astype(bf16), second_new.astype(bf16)


def fold_rows(value):
    rows = value.shape[0]
    out = value[0:8]
    for r in range(8, rows, 8):
        out = jnp.maximum(out, value[r : r + 8])
    return out


def lanes_of(rows_value, first_lane):
    spread = jnp.broadcast_to(rows_value, (16, TILE))
    hit = iota2((16, TILE), 1) == iota2((16, TILE), 0) + first_lane
    return jnp.max(jnp.where(hit, spread, 0.0), axis=0, keepdims=True)


def blocks_of(row, first_lane):
    spread = jnp.broadcast_to(row, (16, TILE))
    hit = iota2((16, TILE), 1) == iota2((16, TILE), 0) + first_lane
    return jnp.max(jnp.where(hit, spread, 0.0), axis=1, keepdims=True)


def step_kernel(
    step_count,
    owner_hbm,
    w_hbm,
    m_hbm,
    v_hbm,
    g_hbm,
    lw_hbm,
    lm_hbm,
    lv_hbm,
    lg_hbm,
    w_out,
    m_out,
    v_out,
    served,
    rows_all,
    lw_out,
    lm_out,
    lv_out,
    lat,
    w_in,
    m_in,
    v_in,
    g_in,
    lw_in,
    lm_in,
    lv_in,
    lg_in,
    w_blocks,
    send,
    own_fold,
    next_fold,
    prev_fold,
    own_scale,
    own_recip,
    next_recip,
    prev_recip,
    next_scale,
    lfold_a,
    lfold_b,
    lrow_out,
    lrow_in,
    edge_out,
    edge_in,
    rows_out,
    lflat,
    lscaled,
    lnear,
    owner,
    inverse,
    in_sem,
    bulk_send,
    bulk_recv,
    lrow_send,
    lrow_recv,
    edge_send,
    edge_recv,
    near_send,
    near_recv,
    rows_send,
    rows_recv,
    ring_send,
    ring_recv,
):
    x = lax.axis_index("dp_0")
    y = lax.axis_index("dp_1")
    c = lax.axis_index("dp_2")
    z = lax.axis_index("expert")
    dp = (x * 4 + y) * 2 + c
    inner = lax.rem(y, 2) * 2 + c
    quad = lax.div(y, 2) * 2
    half = lax.div(x, 2)
    slot = lax.rem(dp, 16)
    is_self = c == half

    def dp_device(target, target_z):
        return (lax.div(target, 8), lax.rem(lax.div(target, 2), 4), lax.rem(target, 2), target_z)

    def quad_device(place, target_z):
        return (x, quad + lax.div(place, 2), lax.rem(place, 2), target_z)

    def up(value, n):
        return lax.rem(value, n)

    place = inner * 8 + z

    def group_device(d):
        other = up(place + d, GROUP)
        return quad_device(lax.div(other, 8), up(other, 8))

    inner_next = up(inner + 1, 4)
    inner_prev = up(inner + 3, 4)

    loads = []

    def load(src, dst):
        copy = pltpu.make_async_copy(src, dst, in_sem.at[len(loads)])
        copy.start()
        loads.append(copy)

    for src, dst in ((lw_hbm, lw_in), (lm_hbm, lm_in), (lv_hbm, lv_in), (lg_hbm, lg_in)):
        load(src, dst)
    slabs = [pl.multiple_of(up(inner + j, 7) * SUB, SUB) for j in range(4, 7)]
    local = pl.multiple_of(inner * SUB, SUB)
    pairs = ((w_hbm, w_in), (m_hbm, m_in), (v_hbm, v_in), (g_hbm, g_in))
    for src, dst in pairs:
        load(src.at[pl.ds(local, TILE), :], dst.at[pl.ds(local, TILE), :])
    for src, dst in pairs:
        for s in slabs:
            load(src.at[pl.ds(s, SUB), :], dst.at[pl.ds(s, SUB), :])

    load(owner_hbm, owner)

    barrier = pltpu.get_barrier_semaphore()

    def greet(device):
        pl.semaphore_signal(barrier, inc=1, device_id=device, device_id_type=MESH)

    @pl.loop(1, GROUP)
    def _(d):
        greet(group_device(d))
        greet(dp_device(up(dp + d, GROUP), z))

    steps = jnp.full((8, TILE), step_count[0], jnp.int32).astype(f32)
    num_scale = (LEARN_RATE / (1.0 - jnp.power(jnp.full((8, TILE), BETA_ONE, f32), steps)))[0:1]
    den_scale = (1.0 / (1.0 - jnp.power(jnp.full((8, TILE), BETA_TWO, f32), steps)))[0:1]

    for copy in loads[:4]:
        copy.wait()
    lat_rows = iota2((LROWS, TILE), 0)

    def lat_blocks(origin):
        start = (inner * 8 + origin) * LROWS
        return LANE0 + lax.div(start, TILE) * LBLOCKS, lat_rows < TILE - lax.rem(start, TILE)

    first_lane, in_first = lat_blocks(z)

    for b in range(LBLOCKS):
        cols = pl.ds(b * TILE, TILE)
        w1, m1, v1 = adamw(
            lw_in[:, cols], lm_in[:, cols], lv_in[:, cols], lg_in[:, cols], num_scale, den_scale
        )
        lw_out[:, cols] = w1
        lflat[b * LROWS : (b + 1) * LROWS, :] = w1
        lm_out[:, cols] = m1
        lv_out[:, cols] = v1
        size = jnp.abs(w1)
        lfold_a[b : b + 1, :] = jnp.max(
            jnp.where(in_first, size, 0.0), axis=0, keepdims=True
        )
        lfold_b[b : b + 1, :] = jnp.max(
            jnp.where(in_first, 0.0, size), axis=0, keepdims=True
        )
    real = iota2((16, 1), 0) < LBLOCKS
    max_a = jnp.where(real, jnp.max(lfold_a[...], axis=1, keepdims=True), 0.0)
    max_b = jnp.where(real, jnp.max(lfold_b[...], axis=1, keepdims=True), 0.0)
    lrow = jnp.maximum(lanes_of(max_a, first_lane), lanes_of(max_b, first_lane + LBLOCKS))
    lrow_out[0] = lrow
    lrow_in[place] = lrow

    def widest(fold):
        return jnp.max(jnp.max(fold[...], axis=1), axis=1, keepdims=True)

    loads[20].wait()

    @pl.loop(0, 16)
    def _(k):
        p = up(x + lax.div(k, 4), 4) * 4 + up(y + lax.rem(k, 4), 4)
        total = jnp.int32(0)
        for b in range(BLOCKS):
            total = jnp.maximum(total, jnp.where(owner[b] == p, b, 0))
        inverse[k] = total

    for copy in loads[4:8]:
        copy.wait()
    own = pl.ds(local, TILE)

    @pl.loop(0, BLOCKS)
    def _(b):
        cols = pl.ds(pl.multiple_of(b * TILE, TILE), TILE)
        w1, m1, v1 = adamw(
            w_in[own, cols], m_in[own, cols], v_in[own, cols], g_in[own, cols], num_scale, den_scale
        )
        w_out[own, cols] = w1
        w_blocks[b, own, :] = w1
        m_out[own, cols] = m1
        v_out[own, cols] = v1
        own_fold[b] = fold_rows(jnp.abs(w1))

    def spread(scale):
        return jnp.broadcast_to(scale, (16, TILE))

    def recip(scale):
        return spread(1.0 / (scale + SCALE_EPS))

    def put(ref, value):
        for b in range(BLOCKS):
            ref[b] = value[b : b + 1]

    own_max = widest(own_fold)
    put(own_scale, spread(own_max))
    put(own_recip, recip(own_max))

    def target(k):
        return (up(x + lax.div(k, 4), 4), up(y + lax.rem(k, 4), 4), half, z)

    def bulk_start(k, rows, count):
        pltpu.make_async_remote_copy(
            src_ref=send.at[k, pl.ds(rows, count), :],
            dst_ref=served.at[slot, pl.ds(rows, count), :],
            send_sem=bulk_send,
            recv_sem=bulk_recv,
            device_id=target(k),
            device_id_type=MESH,
        ).start()

    def bulk_home(rows, count):
        @pl.when(is_self)
        def _():
            served[slot, pl.ds(rows, count), :] = send[0, pl.ds(rows, count), :]

        @pl.when(jnp.logical_not(is_self))
        def _():
            bulk_start(0, rows, count)

    @pl.loop(0, 16)
    def _(k):
        b = inverse[k]
        send[k, own, :] = (w_blocks[b, own, :] * own_recip[b]).astype(bf16)

    pl.semaphore_wait(barrier, 2 * (GROUP - 1))

    @pl.loop(1, GROUP)
    def _(d):
        pltpu.make_async_remote_copy(
            src_ref=lrow_out.at[0],
            dst_ref=lrow_in.at[place],
            send_sem=lrow_send,
            recv_sem=lrow_recv,
            device_id=group_device(d),
            device_id_type=MESH,
        ).start()

    near = [
        pltpu.make_async_remote_copy(
            src_ref=lflat,
            dst_ref=lnear.at[way],
            send_sem=near_send.at[way],
            recv_sem=near_recv.at[way],
            device_id=(x, y, c, up(z + step, 8)),
            device_id_type=MESH,
        )
        for way, step in ((0, 1), (1, 7))
    ]
    for copy in near:
        copy.start()

    @pl.loop(1, 16)
    def _(k):
        bulk_start(k, local, TILE)

    bulk_home(local, TILE)

    for copy in loads[8:20]:
        copy.wait()

    @pl.loop(0, BLOCKS)
    def _(b):
        cols = pl.ds(pl.multiple_of(b * TILE, TILE), TILE)
        after = jnp.zeros((8, TILE), f32)
        before = jnp.zeros((8, TILE), f32)
        for j, s in zip(range(4, 7), slabs):
            rows = pl.ds(s, SUB)
            w1, m1, v1 = adamw(
                w_in[rows, cols], m_in[rows, cols], v_in[rows, cols], g_in[rows, cols],
                num_scale, den_scale,
            )
            w_out[rows, cols] = w1
            w_blocks[b, rows, :] = w1
            m_out[rows, cols] = m1
            v_out[rows, cols] = v1
            size = fold_rows(jnp.abs(w1))
            is_after = inner + j < 7
            after = jnp.maximum(after, jnp.where(is_after, size, 0.0))
            before = jnp.maximum(before, jnp.where(is_after, 0.0, size))
        next_fold[b] = after
        prev_fold[b] = before

    edge_out[0] = lanes_of(widest(next_fold), 0)
    edge_out[1] = lanes_of(widest(prev_fold), 0)

    def edge_copy(n, place):
        return pltpu.make_async_remote_copy(
            src_ref=edge_out.at[n],
            dst_ref=edge_in.at[n],
            send_sem=edge_send.at[n],
            recv_sem=edge_recv.at[n],
            device_id=quad_device(place, z),
            device_id_type=MESH,
        )

    edges = [edge_copy(0, inner_next), edge_copy(1, inner_prev)]
    for copy in edges:
        copy.start()

    for copy in edges:
        copy.wait_recv()
    prev_max = blocks_of(jnp.maximum(edge_out[1], edge_in[0]), 0)
    next_max = blocks_of(jnp.maximum(edge_out[0], edge_in[1]), 0)
    put(prev_recip, recip(prev_max))
    put(next_recip, recip(next_max))
    put(next_scale, spread(next_max))

    @pl.loop(0, 16)
    def _(k):
        b = inverse[k]
        after = next_recip[b]
        before = prev_recip[b]
        for j, s in zip(range(4, 7), slabs):
            rows = pl.ds(s, SUB)
            scale = jnp.where(inner + j < 7, after, before)
            send[k, rows, :] = (w_blocks[b, rows, :] * scale).astype(bf16)

    few_rows = lrow_in.at[pl.ds(0, GROUP - 1)]
    pltpu.make_async_copy(few_rows, few_rows, lrow_recv).wait()
    lmax = jnp.max(lrow_in[...], axis=0)

    lane = iota2((1, TILE), 1)
    scale_lane = 7 * lax.div(slot, 4) + 2 * inner
    lat_lanes = jnp.where(lane >= LANE0, lmax, 0.0)

    def message(k):
        b = inverse[k]
        value = jnp.where(lane == scale_lane, own_scale[b], lat_lanes)
        both = jnp.logical_and(lane == scale_lane + 1, inner < 3)
        return jnp.where(both, next_scale[b], value)

    @pl.loop(0, 16)
    def _(k):
        rows_out[k] = message(k)

    def rows_copy(k, core):
        return pltpu.make_async_remote_copy(
            src_ref=rows_out.at[k],
            dst_ref=rows_all.at[dp],
            send_sem=rows_send,
            recv_sem=rows_recv,
            device_id=(up(x + lax.div(k, 4), 4), up(y + lax.rem(k, 4), 4), core, z),
            device_id_type=MESH,
        )

    rows_all[dp] = rows_out[0]
    rows_copy(0, 1 - c).start()

    @pl.loop(1, 16)
    def _(k):
        rows_copy(k, 0).start()
        rows_copy(k, 1).start()


    def lat_scale(src, origin):
        lane_a, in_a = lat_blocks(origin)
        scale_a = recip(blocks_of(lmax, lane_a))
        scale_b = recip(blocks_of(lmax, lane_a + LBLOCKS))
        for b in range(LBLOCKS):
            rows = slice(b * LROWS, (b + 1) * LROWS)
            scale = jnp.where(in_a, scale_a[b : b + 1, :], scale_b[b : b + 1, :])
            lscaled[rows, :] = src[rows, :] * scale
        lat[origin] = lscaled[...].astype(bf16)

    def ring_copy(way, hop, part):
        origin = up(z + 8 - hop, 8) if way == 0 else up(z + hop, 8)
        peer = up(z + 1, 8) if way == 0 else up(z + 7, 8)
        view = lat.at[origin, pl.ds(part * PART, PART), :]
        n = (way * 4 + hop) * PARTS + part
        return pltpu.make_async_remote_copy(
            src_ref=view,
            dst_ref=view,
            send_sem=ring_send.at[n],
            recv_sem=ring_recv.at[n],
            device_id=(x, y, c, peer),
            device_id_type=MESH,
        )

    def arrived(way, hop, part):
        origin = up(z + 7 - hop, 8) if way == 0 else up(z + 1 + hop, 8)
        view = lat.at[origin, pl.ds(part * PART, PART), :]
        n = (way * 4 + hop) * PARTS + part
        pltpu.make_async_copy(view, view, ring_recv.at[n]).wait()

    hops = [
        (way, hop, part)
        for hop in range(1, 4)
        for part in range(PARTS)
        for way in range(2)
        if hop < 3 or part == way
    ]
    sent = []

    def ring_start(way, hop, part):
        copy = ring_copy(way, hop, part)
        copy.start()
        sent.append(copy)

    for way, origin in ((0, up(z + 7, 8)), (1, up(z + 1, 8))):
        near[way].wait_recv()
        lat_scale(lnear.at[way], origin)
        for part in range(PARTS):
            ring_start(way, 1, part)

    for j, s in zip(range(4, 7), slabs):

        @pl.loop(1, 16)
        def _(k):
            bulk_start(k, s, SUB)

        bulk_home(s, SUB)

    lat_scale(lflat, z)

    for way, hop, part in hops:
        arrived(way, hop, part)
        if (way, hop + 1, part) in hops:
            ring_start(way, hop + 1, part)

    for copy in sent:
        copy.wait_send()
    for copy in edges:
        copy.wait_send()
    for copy in near:
        copy.wait_send()
    pltpu.make_async_copy(few_rows, few_rows, lrow_send).wait()
    few = rows_all.at[pl.ds(0, 31)]
    pltpu.make_async_copy(few, few, rows_send).wait()
    pltpu.make_async_copy(few, few, rows_recv).wait()

    @pl.when(is_self)
    def _():
        rest = served.at[pl.ds(0, 15)]
        pltpu.make_async_copy(rest, rest, bulk_send).wait()
        pltpu.make_async_copy(rest, rest, bulk_recv).wait()

    @pl.when(jnp.logical_not(is_self))
    def _():
        pltpu.make_async_copy(served, served, bulk_send).wait()
        pltpu.make_async_copy(served, served, bulk_recv).wait()


def store_kernel(
    w_in,
    m_in,
    v_in,
    served_in,
    rows_in,
    lw_in,
    lm_in,
    lv_in,
    lat_in,
    w_hbm,
    m_hbm,
    v_hbm,
    served_hbm,
    scales_hbm,
    lw_hbm,
    lm_hbm,
    lv_hbm,
    lserved_hbm,
    lscales_hbm,
    lserved,
    ltall,
    lflat,
    scales,
    lscales,
    lscales_tall,
    sem,
):
    copies = []

    def store(src, dst):
        copy = pltpu.make_async_copy(src, dst, sem.at[len(copies)])
        copy.start()
        copies.append(copy)

    for src, dst in (
        (w_in, w_hbm),
        (m_in, m_hbm),
        (v_in, v_hbm),
        (served_in, served_hbm),
        (lw_in, lw_hbm),
        (lm_in, lm_hbm),
        (lv_in, lv_hbm),
    ):
        store(src, dst)
    for o in range(8):
        lflat[...] = lat_in[o].astype(f32)
        for b in range(LBLOCKS):
            ltall[o * LROWS : (o + 1) * LROWS, b * TILE : (b + 1) * TILE] = lflat[
                b * LROWS : (b + 1) * LROWS, :
            ]
    lserved[...] = ltall[...].astype(bf16)
    store(lserved, lserved_hbm)
    c = lax.axis_index("dp_2")
    mine = jnp.max(rows_in[pl.ds(c * 16, 16)], axis=0)
    scales[...] = mine[:, 0:28]
    for g in range(8):
        group = jnp.max(rows_in[4 * g : 4 * g + 4], axis=0)
        for r in range(7):
            lane = LANE0 + r * LBLOCKS
            lscales_tall[7 * g + r : 7 * g + r + 1, 0:LBLOCKS] = group[:, lane : lane + LBLOCKS]
    lscales[...] = lscales_tall[...].T[0:LBLOCKS, 0:56]
    store(scales, scales_hbm)
    store(lscales, lscales_hbm)
    for copy in copies:
        copy.wait()


def body(
    expert_master,
    expert_first,
    expert_second,
    expert_grad,
    latent_master,
    latent_first,
    latent_second,
    latent_grad,
    step_count,
    column_owner,
):
    hbm = pl.BlockSpec(memory_space=pltpu.HBM)
    vmem = pl.BlockSpec(memory_space=pltpu.VMEM)
    dma = pltpu.SemaphoreType.DMA
    row = (1, TILE)
    made = pl.pallas_call(
        step_kernel,
        out_shape=(
            pltpu.VMEM((ROWS, COLS), f32),
            pltpu.VMEM((ROWS, COLS), bf16),
            pltpu.VMEM((ROWS, COLS), bf16),
            pltpu.VMEM((16, ROWS, TILE), bf16),
            pltpu.VMEM((32, *row), f32),
            pltpu.VMEM((LROWS, LCOLS), f32),
            pltpu.VMEM((LROWS, LCOLS), bf16),
            pltpu.VMEM((LROWS, LCOLS), bf16),
            pltpu.VMEM((8, LFLAT, TILE), bf16),
        ),
        in_specs=[pl.BlockSpec(memory_space=pltpu.SMEM)] + [hbm] * 9,
        out_specs=(vmem,) * 9,
        scratch_shapes=[
            pltpu.VMEM((ROWS, COLS), f32),
            pltpu.VMEM((ROWS, COLS), bf16),
            pltpu.VMEM((ROWS, COLS), bf16),
            pltpu.VMEM((ROWS, COLS), bf16),
            pltpu.VMEM((LROWS, LCOLS), f32),
            pltpu.VMEM((LROWS, LCOLS), bf16),
            pltpu.VMEM((LROWS, LCOLS), bf16),
            pltpu.VMEM((LROWS, LCOLS), bf16),
            pltpu.VMEM((16, ROWS, TILE), f32),
            pltpu.VMEM((16, ROWS, TILE), bf16),
            pltpu.VMEM((16, 8, TILE), f32),
            pltpu.VMEM((16, 8, TILE), f32),
            pltpu.VMEM((16, 8, TILE), f32),
            pltpu.VMEM((16, *row), f32),
            pltpu.VMEM((16, *row), f32),
            pltpu.VMEM((16, *row), f32),
            pltpu.VMEM((16, *row), f32),
            pltpu.VMEM((16, *row), f32),
            pltpu.VMEM((16, TILE), f32),
            pltpu.VMEM((16, TILE), f32),
            pltpu.VMEM((1, *row), f32),
            pltpu.VMEM((GROUP, *row), f32),
            pltpu.VMEM((2, *row), f32),
            pltpu.VMEM((2, *row), f32),
            pltpu.VMEM((16, *row), f32),
            pltpu.VMEM((LFLAT, TILE), f32),
            pltpu.VMEM((LFLAT, TILE), f32),
            pltpu.VMEM((2, LFLAT, TILE), f32),
            pltpu.SMEM((16,), jnp.int32),
            pltpu.SMEM((16,), jnp.int32),
            dma((21,)),
            dma,
            dma,
            dma,
            dma,
            dma((2,)),
            dma((2,)),
            dma((2,)),
            dma((2,)),
            dma,
            dma,
            dma((8 * PARTS,)),
            dma((8 * PARTS,)),
        ],
        compiler_params=pltpu.CompilerParams(
            collective_id=0, has_side_effects=True, vmem_limit_bytes=24 << 20
        ),
        name="step",
    )(
        pltpu.with_memory_space_constraint(step_count, pltpu.SMEM),
        *(
            pltpu.with_memory_space_constraint(value, pltpu.HBM)
            for value in (
                column_owner,
                expert_master[0],
                expert_first[0],
                expert_second[0],
                expert_grad[0],
                latent_master,
                latent_first,
                latent_second,
                latent_grad,
            )
        ),
    )
    out = pl.pallas_call(
        store_kernel,
        out_shape=(
            jax.ShapeDtypeStruct((ROWS, COLS), f32),
            jax.ShapeDtypeStruct((ROWS, COLS), bf16),
            jax.ShapeDtypeStruct((ROWS, COLS), bf16),
            jax.ShapeDtypeStruct((16, ROWS, TILE), bf16),
            jax.ShapeDtypeStruct((1, 28), f32),
            jax.ShapeDtypeStruct((LROWS, LCOLS), f32),
            jax.ShapeDtypeStruct((LROWS, LCOLS), bf16),
            jax.ShapeDtypeStruct((LROWS, LCOLS), bf16),
            jax.ShapeDtypeStruct((ROWS, LCOLS), bf16),
            jax.ShapeDtypeStruct((LBLOCKS, 56), f32),
        ),
        in_specs=[vmem] * 9,
        out_specs=(hbm,) * 10,
        scratch_shapes=[
            pltpu.VMEM((ROWS, LCOLS), bf16),
            pltpu.VMEM((ROWS, LCOLS), f32),
            pltpu.VMEM((LFLAT, TILE), f32),
            pltpu.VMEM((1, 28), f32),
            pltpu.VMEM((LBLOCKS, 56), f32),
            pltpu.VMEM((TILE, TILE), f32),
            dma((10,)),
        ],
        compiler_params=pltpu.CompilerParams(vmem_limit_bytes=8 << 20),
        name="store",
    )(*made)
    master, first, second, served, scales, lmaster, lfirst, lsecond, lserved, lscales = out
    return (
        master[None],
        first[None],
        second[None],
        served.reshape(1, 16 * ROWS, TILE),
        scales,
        lmaster,
        lfirst,
        lsecond,
        lserved,
        lscales.T,
    )


def solution(mesh):
    torus = Mesh(
        mesh.devices.reshape(4, 4, 2, mesh.shape["expert"]), ("dp_0", "dp_1", "dp_2", "expert")
    )
    expert = P("expert", DP, None)
    latent = P(DP_EXPERT, None)
    return jax.shard_map(
        body,
        mesh=torus,
        in_specs=(expert,) * 4 + (latent,) * 4 + (P(), P()),
        out_specs=(
            expert,
            expert,
            expert,
            expert,
            P("expert", DP),
            latent,
            latent,
            latent,
            P(DP, None),
            P(),
        ),
        check_vma=False,
    )
```

```python
import jax
import jax.numpy as jnp
from jax import lax
from jax.experimental import pallas as pl
from jax.experimental.pallas import tpu as pltpu
from jax.sharding import Mesh
from jax.sharding import PartitionSpec as P

MESH = pl.DeviceIdType.MESH
TILE = 128
DP = ("dp_0", "dp_1", "dp_2")
DP_EXPERT = ("dp_0", "dp_1", "dp_2", "expert")

BETA_ONE = 0.9
BETA_TWO = 0.95
LEARN_RATE = 0.2
DECAY_RATE = 0.1
ADAM_EPS = 1e-08
SCALE_EPS = 1e-06

ROWS = 224
COLS = 2048
BLOCKS = COLS // TILE
SUB = 32
LROWS = 28
LCOLS = 1536
LBLOCKS = LCOLS // TILE
LFLAT = LROWS * LBLOCKS
PARTS = 2
PART = LFLAT // PARTS
GROUP = 32

f32 = jnp.float32
bf16 = jnp.bfloat16


def iota2(shape, dim):
    return lax.broadcasted_iota(jnp.int32, shape, dim)


def adamw(master, first, second, grad, num_scale, den_scale):
    g = grad.astype(f32)
    first_new = BETA_ONE * first.astype(f32) + (1.0 - BETA_ONE) * g
    second_new = BETA_TWO * second.astype(f32) + (1.0 - BETA_TWO) * g * g
    update = (first_new * num_scale) / (jnp.sqrt(second_new * den_scale) + ADAM_EPS)
    master_new = (1.0 - LEARN_RATE * DECAY_RATE) * master - update
    return master_new, first_new.astype(bf16), second_new.astype(bf16)


def fold_rows(value):
    rows = value.shape[0]
    out = value[0:8]
    for r in range(8, rows, 8):
        out = jnp.maximum(out, value[r : r + 8])
    return out


def lanes_of(rows_value, first_lane):
    spread = jnp.broadcast_to(rows_value, (16, TILE))
    hit = iota2((16, TILE), 1) == iota2((16, TILE), 0) + first_lane
    return jnp.max(jnp.where(hit, spread, 0.0), axis=0, keepdims=True)


def blocks_of(row, first_lane):
    spread = jnp.broadcast_to(row, (16, TILE))
    hit = iota2((16, TILE), 1) == iota2((16, TILE), 0) + first_lane
    return jnp.max(jnp.where(hit, spread, 0.0), axis=1, keepdims=True)


def step_kernel(
    step_count,
    owner_hbm,
    w_hbm,
    m_hbm,
    v_hbm,
    g_hbm,
    lw_hbm,
    lm_hbm,
    lv_hbm,
    lg_hbm,
    w_out,
    m_out,
    v_out,
    served,
    rows_all,
    groups_all,
    lw_out,
    lm_out,
    lv_out,
    lat,
    w_in,
    m_in,
    v_in,
    g_in,
    lw_in,
    lm_in,
    lv_in,
    lg_in,
    w_blocks,
    send,
    own_fold,
    next_fold,
    prev_fold,
    own_scale,
    own_recip,
    next_recip,
    prev_recip,
    next_scale,
    lfold_a,
    lfold_b,
    lrow_out,
    lrow_in,
    edge_out,
    edge_in,
    rows_out,
    groups_out,
    lflat,
    lscaled,
    lnear,
    owner,
    inverse,
    in_sem,
    bulk_send,
    bulk_recv,
    lrow_send,
    lrow_recv,
    edge_send,
    edge_recv,
    near_send,
    near_recv,
    rows_send,
    rows_recv,
    groups_send,
    groups_recv,
    ring_send,
    ring_recv,
):
    x = lax.axis_index("dp_0")
    y = lax.axis_index("dp_1")
    c = lax.axis_index("dp_2")
    z = lax.axis_index("expert")
    dp = (x * 4 + y) * 2 + c
    inner = lax.rem(y, 2) * 2 + c
    quad = lax.div(y, 2) * 2
    half = lax.div(x, 2)
    slot = lax.rem(dp, 16)
    is_self = c == half

    xs = [lax.rem(x + d, 4) for d in range(4)]
    ys = [lax.rem(y + d, 4) for d in range(4)]
    zs = [lax.rem(z + d, 8) for d in range(8)]
    cs = [c, 1 - c]
    quads = [lax.rem(inner + d, 4) for d in range(4)]
    quads = [(quad + lax.div(n, 2), lax.rem(n, 2)) for n in quads]
    place = inner * 8 + z

    def up(value, n):
        return lax.rem(value, n)

    def far(d, n):
        return min(d, n - d)

    def target(k):
        return (xs[k // 4], ys[k % 4], half, z)

    group_devices = sorted(
        ((di, dz) for di in range(4) for dz in range(8) if di or dz), key=lambda d: -far(d[1], 8)
    )
    group_devices = [(x, *quads[di], zs[dz]) for di, dz in group_devices]
    near_y = 1 - 2 * lax.rem(y, 2)
    plane_devices = [
        (xs[dx], lax.rem(y + 4 + near_y * dy, 4), cs[dc], z)
        for dx in (2, 1, 3, 0)
        for dy in (2, 3, 1, 0)
        for dc in range(2)
        if dx or dy > 1
    ]

    barrier = pltpu.get_barrier_semaphore()
    for device in group_devices + plane_devices:
        pl.semaphore_signal(barrier, inc=1, device_id=device, device_id_type=MESH)

    loads = []

    def load(src, dst):
        copy = pltpu.make_async_copy(src, dst, in_sem.at[len(loads)])
        copy.start()
        loads.append(copy)

    for src, dst in ((lw_hbm, lw_in), (lm_hbm, lm_in), (lv_hbm, lv_in), (lg_hbm, lg_in)):
        load(src, dst)
    slabs = [pl.multiple_of(up(inner + j, 7) * SUB, SUB) for j in range(4, 7)]
    local = pl.multiple_of(inner * SUB, SUB)
    pairs = ((w_hbm, w_in), (m_hbm, m_in), (v_hbm, v_in), (g_hbm, g_in))
    for src, dst in pairs:
        load(src.at[pl.ds(local, TILE), :], dst.at[pl.ds(local, TILE), :])
    for src, dst in pairs:
        for s in slabs:
            load(src.at[pl.ds(s, SUB), :], dst.at[pl.ds(s, SUB), :])

    load(owner_hbm, owner)

    steps = jnp.full((8, TILE), step_count[0], jnp.int32).astype(f32)
    num_scale = (LEARN_RATE / (1.0 - jnp.power(jnp.full((8, TILE), BETA_ONE, f32), steps)))[0:1]
    den_scale = (1.0 / (1.0 - jnp.power(jnp.full((8, TILE), BETA_TWO, f32), steps)))[0:1]

    for copy in loads[:4]:
        copy.wait()
    lat_rows = iota2((LROWS, TILE), 0)

    def lat_blocks(origin):
        start = (inner * 8 + origin) * LROWS
        return lax.div(start, TILE) * LBLOCKS, lat_rows < TILE - lax.rem(start, TILE)

    first_lane, in_first = lat_blocks(z)

    for b in range(LBLOCKS):
        cols = pl.ds(b * TILE, TILE)
        w1, m1, v1 = adamw(
            lw_in[:, cols], lm_in[:, cols], lv_in[:, cols], lg_in[:, cols], num_scale, den_scale
        )
        lw_out[:, cols] = w1
        lflat[b * LROWS : (b + 1) * LROWS, :] = w1
        lm_out[:, cols] = m1
        lv_out[:, cols] = v1
        size = jnp.abs(w1)
        lfold_a[b : b + 1, :] = jnp.max(
            jnp.where(in_first, size, 0.0), axis=0, keepdims=True
        )
        lfold_b[b : b + 1, :] = jnp.max(
            jnp.where(in_first, 0.0, size), axis=0, keepdims=True
        )
    real = iota2((16, 1), 0) < LBLOCKS
    max_a = jnp.where(real, jnp.max(lfold_a[...], axis=1, keepdims=True), 0.0)
    max_b = jnp.where(real, jnp.max(lfold_b[...], axis=1, keepdims=True), 0.0)
    lrow = jnp.maximum(lanes_of(max_a, first_lane), lanes_of(max_b, first_lane + LBLOCKS))
    lrow_out[0] = lrow
    lrow_in[place] = lrow

    def widest(fold):
        return jnp.max(jnp.max(fold[...], axis=1), axis=1, keepdims=True)

    loads[20].wait()

    @pl.loop(0, 16)
    def _(k):
        p = up(x + lax.div(k, 4), 4) * 4 + up(y + lax.rem(k, 4), 4)
        total = jnp.int32(0)
        for b in range(BLOCKS):
            total = jnp.maximum(total, jnp.where(owner[b] == p, b, 0))
        inverse[k] = total

    for copy in loads[4:8]:
        copy.wait()
    own = pl.ds(local, TILE)

    @pl.loop(0, BLOCKS)
    def _(b):
        cols = pl.ds(pl.multiple_of(b * TILE, TILE), TILE)
        w1, m1, v1 = adamw(
            w_in[own, cols], m_in[own, cols], v_in[own, cols], g_in[own, cols], num_scale, den_scale
        )
        w_out[own, cols] = w1
        w_blocks[b, own, :] = w1
        m_out[own, cols] = m1
        v_out[own, cols] = v1
        own_fold[b] = fold_rows(jnp.abs(w1))

    def spread(scale):
        return jnp.broadcast_to(scale, (16, TILE))

    def recip(scale):
        return spread(1.0 / (scale + SCALE_EPS))

    def put(ref, value):
        for b in range(BLOCKS):
            ref[b] = value[b : b + 1]

    own_max = widest(own_fold)
    put(own_scale, spread(own_max))
    put(own_recip, recip(own_max))

    def bulk_start(k, rows, count):
        pltpu.make_async_remote_copy(
            src_ref=send.at[k, pl.ds(rows, count), :],
            dst_ref=served.at[slot, pl.ds(rows, count), :],
            send_sem=bulk_send,
            recv_sem=bulk_recv,
            device_id=target(k),
            device_id_type=MESH,
        ).start()

    def bulk_home(rows, count):
        @pl.when(is_self)
        def _():
            served[slot, pl.ds(rows, count), :] = send[0, pl.ds(rows, count), :]

        @pl.when(jnp.logical_not(is_self))
        def _():
            bulk_start(0, rows, count)

    @pl.loop(0, 16)
    def _(k):
        b = inverse[k]
        send[k, own, :] = (w_blocks[b, own, :] * own_recip[b]).astype(bf16)

    pl.semaphore_wait(barrier, len(group_devices) + len(plane_devices))

    for device in group_devices:
        pltpu.make_async_remote_copy(
            src_ref=lrow_out.at[0],
            dst_ref=lrow_in.at[place],
            send_sem=lrow_send,
            recv_sem=lrow_recv,
            device_id=device,
            device_id_type=MESH,
        ).start()

    near = [
        pltpu.make_async_remote_copy(
            src_ref=lflat,
            dst_ref=lnear.at[way],
            send_sem=near_send.at[way],
            recv_sem=near_recv.at[way],
            device_id=(x, y, c, zs[step]),
            device_id_type=MESH,
        )
        for way, step in ((0, 1), (1, 7))
    ]
    for copy in near:
        copy.start()

    for k in range(4, 16):
        bulk_start(k, local, TILE)

    for copy in loads[8:20]:
        copy.wait()

    @pl.loop(0, BLOCKS)
    def _(b):
        cols = pl.ds(pl.multiple_of(b * TILE, TILE), TILE)
        after = jnp.zeros((8, TILE), f32)
        before = jnp.zeros((8, TILE), f32)
        for j, s in zip(range(4, 7), slabs):
            rows = pl.ds(s, SUB)
            w1, m1, v1 = adamw(
                w_in[rows, cols], m_in[rows, cols], v_in[rows, cols], g_in[rows, cols],
                num_scale, den_scale,
            )
            w_out[rows, cols] = w1
            w_blocks[b, rows, :] = w1
            m_out[rows, cols] = m1
            v_out[rows, cols] = v1
            size = fold_rows(jnp.abs(w1))
            is_after = inner + j < 7
            after = jnp.maximum(after, jnp.where(is_after, size, 0.0))
            before = jnp.maximum(before, jnp.where(is_after, 0.0, size))
        next_fold[b] = after
        prev_fold[b] = before

    edge_out[0] = lanes_of(widest(next_fold), 0)
    edge_out[1] = lanes_of(widest(prev_fold), 0)

    def edge_copy(n, step):
        return pltpu.make_async_remote_copy(
            src_ref=edge_out.at[n],
            dst_ref=edge_in.at[n],
            send_sem=edge_send.at[n],
            recv_sem=edge_recv.at[n],
            device_id=(x, *quads[step], z),
            device_id_type=MESH,
        )

    edges = [edge_copy(0, 1), edge_copy(1, 3)]
    for copy in edges:
        copy.start()
    for k in range(1, 4):
        bulk_start(k, local, TILE)
    bulk_home(local, TILE)

    for copy in edges:
        copy.wait_recv()
    prev_max = blocks_of(jnp.maximum(edge_out[1], edge_in[0]), 0)
    next_max = blocks_of(jnp.maximum(edge_out[0], edge_in[1]), 0)
    put(prev_recip, recip(prev_max))
    put(next_recip, recip(next_max))
    put(next_scale, spread(next_max))

    lane = iota2((1, TILE), 1)
    scale_lane = 7 * lax.div(slot, 4) + 2 * inner
    takes_next = jnp.logical_and(lane == scale_lane + 1, inner < 3)

    @pl.loop(0, 16)
    def _(k):
        b = inverse[k]
        value = jnp.where(lane == scale_lane, own_scale[b], 0.0)
        rows_out[k] = jnp.where(takes_next, next_scale[b], value)
        after = next_recip[b]
        before = prev_recip[b]
        for j, s in zip(range(4, 7), slabs):
            rows = pl.ds(s, SUB)
            scale = jnp.where(inner + j < 7, after, before)
            send[k, rows, :] = (w_blocks[b, rows, :] * scale).astype(bf16)

    def rows_start(k):
        pltpu.make_async_remote_copy(
            src_ref=rows_out.at[k],
            dst_ref=rows_all.at[slot],
            send_sem=rows_send,
            recv_sem=rows_recv,
            device_id=target(k),
            device_id_type=MESH,
        ).start()

    for k in range(1, 16):
        rows_start(k)

    @pl.when(is_self)
    def _():
        rows_all[slot] = rows_out[0]

    @pl.when(jnp.logical_not(is_self))
    def _():
        rows_start(0)

    few_rows = lrow_in.at[pl.ds(0, GROUP - 1)]
    pltpu.make_async_copy(few_rows, few_rows, lrow_recv).wait()
    lmax = jnp.max(lrow_in[...], axis=0)
    group = 2 * x + lax.div(y, 2)
    groups_out[0] = lmax
    groups_all[group] = lmax

    for dx, dy in [(dx, dy) for dx in range(4) for dy in (0, 2) if dx or dy]:
        pltpu.make_async_remote_copy(
            src_ref=groups_out.at[0],
            dst_ref=groups_all.at[group],
            send_sem=groups_send,
            recv_sem=groups_recv,
            device_id=(xs[dx], ys[dy], c, z),
            device_id_type=MESH,
        ).start()

    def shared_start(n):
        pieces = [(0, n * SUB), (n * SUB + TILE, ROWS - n * SUB - TILE)]

        @pl.when(inner == n)
        def _():
            for rows, count in pieces:
                if count:
                    for k in range(1, 16):
                        bulk_start(k, rows, count)
                    bulk_home(rows, count)

    def lat_scale(src, origin):
        lane_a, in_a = lat_blocks(origin)
        scale_a = recip(blocks_of(lmax, lane_a))
        scale_b = recip(blocks_of(lmax, lane_a + LBLOCKS))
        for b in range(LBLOCKS):
            rows = slice(b * LROWS, (b + 1) * LROWS)
            scale = jnp.where(in_a, scale_a[b : b + 1, :], scale_b[b : b + 1, :])
            lscaled[rows, :] = src[rows, :] * scale
        lat[origin] = lscaled[...].astype(bf16)

    def ring_copy(way, hop, part):
        origin = up(z + 8 - hop, 8) if way == 0 else up(z + hop, 8)
        peer = up(z + 1, 8) if way == 0 else up(z + 7, 8)
        view = lat.at[origin, pl.ds(part * PART, PART), :]
        n = (way * 4 + hop) * PARTS + part
        return pltpu.make_async_remote_copy(
            src_ref=view,
            dst_ref=view,
            send_sem=ring_send.at[n],
            recv_sem=ring_recv.at[n],
            device_id=(x, y, c, peer),
            device_id_type=MESH,
        )

    def arrived(way, hop, part):
        origin = up(z + 7 - hop, 8) if way == 0 else up(z + 1 + hop, 8)
        view = lat.at[origin, pl.ds(part * PART, PART), :]
        n = (way * 4 + hop) * PARTS + part
        pltpu.make_async_copy(view, view, ring_recv.at[n]).wait()

    hops = [
        (way, hop, part)
        for hop in range(1, 4)
        for part in range(PARTS)
        for way in range(2)
        if hop < 3 or part == way
    ]
    sent = []

    def ring_start(way, hop, part):
        copy = ring_copy(way, hop, part)
        copy.start()
        sent.append(copy)

    for way, origin in ((0, up(z + 7, 8)), (1, up(z + 1, 8))):
        near[way].wait_recv()
        lat_scale(lnear.at[way], origin)
        for part in range(PARTS):
            ring_start(way, 1, part)

    for n in range(4):
        shared_start(n)
    lat_scale(lflat, z)

    for way, hop, part in hops:
        arrived(way, hop, part)
        if (way, hop + 1, part) in hops:
            ring_start(way, hop + 1, part)

    for copy in sent:
        copy.wait_send()
    for copy in edges:
        copy.wait_send()
    for copy in near:
        copy.wait_send()
    pltpu.make_async_copy(few_rows, few_rows, lrow_send).wait()
    seven = groups_all.at[pl.ds(0, 7)]
    pltpu.make_async_copy(seven, seven, groups_send).wait()
    pltpu.make_async_copy(seven, seven, groups_recv).wait()

    @pl.when(is_self)
    def _():
        rest = served.at[pl.ds(0, 15)]
        pltpu.make_async_copy(rest, rest, bulk_send).wait()
        pltpu.make_async_copy(rest, rest, bulk_recv).wait()
        rest = rows_all.at[pl.ds(0, 15)]
        pltpu.make_async_copy(rest, rest, rows_send).wait()
        pltpu.make_async_copy(rest, rest, rows_recv).wait()

    @pl.when(jnp.logical_not(is_self))
    def _():
        pltpu.make_async_copy(served, served, bulk_send).wait()
        pltpu.make_async_copy(served, served, bulk_recv).wait()
        pltpu.make_async_copy(rows_all, rows_all, rows_send).wait()
        pltpu.make_async_copy(rows_all, rows_all, rows_recv).wait()


def store_kernel(
    w_in,
    m_in,
    v_in,
    served_in,
    rows_in,
    groups_in,
    lw_in,
    lm_in,
    lv_in,
    lat_in,
    w_hbm,
    m_hbm,
    v_hbm,
    served_hbm,
    scales_hbm,
    lw_hbm,
    lm_hbm,
    lv_hbm,
    lserved_hbm,
    lscales_hbm,
    lserved,
    ltall,
    lflat,
    scales,
    lscales,
    lscales_tall,
    sem,
):
    copies = []

    def store(src, dst):
        copy = pltpu.make_async_copy(src, dst, sem.at[len(copies)])
        copy.start()
        copies.append(copy)

    for src, dst in (
        (w_in, w_hbm),
        (m_in, m_hbm),
        (v_in, v_hbm),
        (served_in, served_hbm),
        (lw_in, lw_hbm),
        (lm_in, lm_hbm),
        (lv_in, lv_hbm),
    ):
        store(src, dst)
    for o in range(8):
        lflat[...] = lat_in[o].astype(f32)
        for b in range(LBLOCKS):
            ltall[o * LROWS : (o + 1) * LROWS, b * TILE : (b + 1) * TILE] = lflat[
                b * LROWS : (b + 1) * LROWS, :
            ]
    lserved[...] = ltall[...].astype(bf16)
    store(lserved, lserved_hbm)
    scales[...] = jnp.max(rows_in[...], axis=0)[:, 0:28]
    for g in range(8):
        group = groups_in[g]
        for r in range(7):
            lane = r * LBLOCKS
            lscales_tall[7 * g + r : 7 * g + r + 1, 0:LBLOCKS] = group[:, lane : lane + LBLOCKS]
    lscales[...] = lscales_tall[...].T[0:LBLOCKS, 0:56]
    store(scales, scales_hbm)
    store(lscales, lscales_hbm)
    for copy in copies:
        copy.wait()


def body(
    expert_master,
    expert_first,
    expert_second,
    expert_grad,
    latent_master,
    latent_first,
    latent_second,
    latent_grad,
    step_count,
    column_owner,
):
    hbm = pl.BlockSpec(memory_space=pltpu.HBM)
    vmem = pl.BlockSpec(memory_space=pltpu.VMEM)
    dma = pltpu.SemaphoreType.DMA
    row = (1, TILE)
    made = pl.pallas_call(
        step_kernel,
        out_shape=(
            pltpu.VMEM((ROWS, COLS), f32),
            pltpu.VMEM((ROWS, COLS), bf16),
            pltpu.VMEM((ROWS, COLS), bf16),
            pltpu.VMEM((16, ROWS, TILE), bf16),
            pltpu.VMEM((16, *row), f32),
            pltpu.VMEM((8, *row), f32),
            pltpu.VMEM((LROWS, LCOLS), f32),
            pltpu.VMEM((LROWS, LCOLS), bf16),
            pltpu.VMEM((LROWS, LCOLS), bf16),
            pltpu.VMEM((8, LFLAT, TILE), bf16),
        ),
        in_specs=[pl.BlockSpec(memory_space=pltpu.SMEM)] + [hbm] * 9,
        out_specs=(vmem,) * 10,
        scratch_shapes=[
            pltpu.VMEM((ROWS, COLS), f32),
            pltpu.VMEM((ROWS, COLS), bf16),
            pltpu.VMEM((ROWS, COLS), bf16),
            pltpu.VMEM((ROWS, COLS), bf16),
            pltpu.VMEM((LROWS, LCOLS), f32),
            pltpu.VMEM((LROWS, LCOLS), bf16),
            pltpu.VMEM((LROWS, LCOLS), bf16),
            pltpu.VMEM((LROWS, LCOLS), bf16),
            pltpu.VMEM((16, ROWS, TILE), f32),
            pltpu.VMEM((16, ROWS, TILE), bf16),
            pltpu.VMEM((16, 8, TILE), f32),
            pltpu.VMEM((16, 8, TILE), f32),
            pltpu.VMEM((16, 8, TILE), f32),
            pltpu.VMEM((16, *row), f32),
            pltpu.VMEM((16, *row), f32),
            pltpu.VMEM((16, *row), f32),
            pltpu.VMEM((16, *row), f32),
            pltpu.VMEM((16, *row), f32),
            pltpu.VMEM((16, TILE), f32),
            pltpu.VMEM((16, TILE), f32),
            pltpu.VMEM((1, *row), f32),
            pltpu.VMEM((GROUP, *row), f32),
            pltpu.VMEM((2, *row), f32),
            pltpu.VMEM((2, *row), f32),
            pltpu.VMEM((16, *row), f32),
            pltpu.VMEM((1, *row), f32),
            pltpu.VMEM((LFLAT, TILE), f32),
            pltpu.VMEM((LFLAT, TILE), f32),
            pltpu.VMEM((2, LFLAT, TILE), f32),
            pltpu.SMEM((16,), jnp.int32),
            pltpu.SMEM((16,), jnp.int32),
            dma((21,)),
            dma,
            dma,
            dma,
            dma,
            dma((2,)),
            dma((2,)),
            dma((2,)),
            dma((2,)),
            dma,
            dma,
            dma,
            dma,
            dma((8 * PARTS,)),
            dma((8 * PARTS,)),
        ],
        compiler_params=pltpu.CompilerParams(
            collective_id=0, has_side_effects=True, vmem_limit_bytes=24 << 20
        ),
        name="step",
    )(
        pltpu.with_memory_space_constraint(step_count, pltpu.SMEM),
        *(
            pltpu.with_memory_space_constraint(value, pltpu.HBM)
            for value in (
                column_owner,
                expert_master[0],
                expert_first[0],
                expert_second[0],
                expert_grad[0],
                latent_master,
                latent_first,
                latent_second,
                latent_grad,
            )
        ),
    )
    out = pl.pallas_call(
        store_kernel,
        out_shape=(
            jax.ShapeDtypeStruct((ROWS, COLS), f32),
            jax.ShapeDtypeStruct((ROWS, COLS), bf16),
            jax.ShapeDtypeStruct((ROWS, COLS), bf16),
            jax.ShapeDtypeStruct((16, ROWS, TILE), bf16),
            jax.ShapeDtypeStruct((1, 28), f32),
            jax.ShapeDtypeStruct((LROWS, LCOLS), f32),
            jax.ShapeDtypeStruct((LROWS, LCOLS), bf16),
            jax.ShapeDtypeStruct((LROWS, LCOLS), bf16),
            jax.ShapeDtypeStruct((ROWS, LCOLS), bf16),
            jax.ShapeDtypeStruct((LBLOCKS, 56), f32),
        ),
        in_specs=[vmem] * 10,
        out_specs=(hbm,) * 10,
        scratch_shapes=[
            pltpu.VMEM((ROWS, LCOLS), bf16),
            pltpu.VMEM((ROWS, LCOLS), f32),
            pltpu.VMEM((LFLAT, TILE), f32),
            pltpu.VMEM((1, 28), f32),
            pltpu.VMEM((LBLOCKS, 56), f32),
            pltpu.VMEM((TILE, TILE), f32),
            dma((10,)),
        ],
        compiler_params=pltpu.CompilerParams(vmem_limit_bytes=8 << 20),
        name="store",
    )(*made)
    master, first, second, served, scales, lmaster, lfirst, lsecond, lserved, lscales = out
    return (
        master[None],
        first[None],
        second[None],
        served.reshape(1, 16 * ROWS, TILE),
        scales,
        lmaster,
        lfirst,
        lsecond,
        lserved,
        lscales.T,
    )


def solution(mesh):
    torus = Mesh(
        mesh.devices.reshape(4, 4, 2, mesh.shape["expert"]), ("dp_0", "dp_1", "dp_2", "expert")
    )
    expert = P("expert", DP, None)
    latent = P(DP_EXPERT, None)
    return jax.shard_map(
        body,
        mesh=torus,
        in_specs=(expert,) * 4 + (latent,) * 4 + (P(), P()),
        out_specs=(
            expert,
            expert,
            expert,
            expert,
            P("expert", DP),
            latent,
            latent,
            latent,
            P(DP, None),
            P(),
        ),
        check_vma=False,
    )
```

```python
import jax
import jax.numpy as jnp
from jax import lax
from jax.experimental import pallas as pl
from jax.experimental.pallas import tpu as pltpu
from jax.sharding import Mesh
from jax.sharding import PartitionSpec as P

MESH = pl.DeviceIdType.MESH
SPREAD = (8, 4, 12, 9, 5, 13, 10, 6, 14, 11, 7, 15, 2, 1, 3)
TILE = 128
DP = ("dp_0", "dp_1", "dp_2")
DP_EXPERT = ("dp_0", "dp_1", "dp_2", "expert")

BETA_ONE = 0.9
BETA_TWO = 0.95
LEARN_RATE = 0.2
DECAY_RATE = 0.1
ADAM_EPS = 1e-08
SCALE_EPS = 1e-06

ROWS = 224
COLS = 2048
BLOCKS = COLS // TILE
SUB = 32
LROWS = 28
LCOLS = 1536
LBLOCKS = LCOLS // TILE
LFLAT = LROWS * LBLOCKS
PARTS = 2
PART = LFLAT // PARTS
GROUP = 32

f32 = jnp.float32
bf16 = jnp.bfloat16


def iota2(shape, dim):
    return lax.broadcasted_iota(jnp.int32, shape, dim)


def adamw(master, first, second, grad, num_scale, den_scale):
    g = grad.astype(f32)
    first_new = BETA_ONE * first.astype(f32) + (1.0 - BETA_ONE) * g
    second_new = BETA_TWO * second.astype(f32) + (1.0 - BETA_TWO) * g * g
    update = (first_new * num_scale) / (jnp.sqrt(second_new * den_scale) + ADAM_EPS)
    master_new = (1.0 - LEARN_RATE * DECAY_RATE) * master - update
    return master_new, first_new.astype(bf16), second_new.astype(bf16)


def fold_rows(value):
    rows = value.shape[0]
    out = value[0:8]
    for r in range(8, rows, 8):
        out = jnp.maximum(out, value[r : r + 8])
    return out


def lanes_of(rows_value, first_lane):
    spread = jnp.broadcast_to(rows_value, (16, TILE))
    hit = iota2((16, TILE), 1) == iota2((16, TILE), 0) + first_lane
    return jnp.max(jnp.where(hit, spread, 0.0), axis=0, keepdims=True)


def blocks_of(row, first_lane):
    spread = jnp.broadcast_to(row, (16, TILE))
    hit = iota2((16, TILE), 1) == iota2((16, TILE), 0) + first_lane
    return jnp.max(jnp.where(hit, spread, 0.0), axis=1, keepdims=True)


def step_kernel(
    step_count,
    owner_hbm,
    w_hbm,
    m_hbm,
    v_hbm,
    g_hbm,
    lw_hbm,
    lm_hbm,
    lv_hbm,
    lg_hbm,
    w_out,
    m_out,
    v_out,
    served,
    rows_all,
    groups_all,
    lw_out,
    lm_out,
    lv_out,
    lat,
    w_in,
    m_in,
    v_in,
    g_in,
    lw_in,
    lm_in,
    lv_in,
    lg_in,
    w_blocks,
    send,
    own_fold,
    next_fold,
    prev_fold,
    own_scale,
    own_recip,
    next_recip,
    prev_recip,
    next_scale,
    lfold_a,
    lfold_b,
    lrow_out,
    lrow_in,
    edge_out,
    edge_in,
    rows_out,
    groups_out,
    lflat,
    lscaled,
    lnear,
    owner,
    inverse,
    in_sem,
    bulk_send,
    bulk_recv,
    lrow_send,
    lrow_recv,
    edge_send,
    edge_recv,
    near_send,
    near_recv,
    rows_send,
    rows_recv,
    groups_send,
    groups_recv,
    ring_send,
    ring_recv,
):
    x = lax.axis_index("dp_0")
    y = lax.axis_index("dp_1")
    c = lax.axis_index("dp_2")
    z = lax.axis_index("expert")
    dp = (x * 4 + y) * 2 + c
    inner = lax.rem(y, 2) * 2 + c
    quad = lax.div(y, 2) * 2
    half = lax.div(x, 2)
    slot = lax.rem(dp, 16)
    is_self = c == half

    xs = [lax.rem(x + d, 4) for d in range(4)]
    ys = [lax.rem(y + d, 4) for d in range(4)]
    zs = [lax.rem(z + d, 8) for d in range(8)]
    cs = [c, 1 - c]
    quads = [lax.rem(inner + d, 4) for d in range(4)]
    quads = [(quad + lax.div(n, 2), lax.rem(n, 2)) for n in quads]
    place = inner * 8 + z

    def up(value, n):
        return lax.rem(value, n)

    def far(d, n):
        return min(d, n - d)

    def target(k):
        return (xs[k // 4], ys[k % 4], half, z)

    group_devices = sorted(
        ((di, dz) for di in range(4) for dz in range(8) if di or dz), key=lambda d: -far(d[1], 8)
    )
    group_devices = [(x, *quads[di], zs[dz]) for di, dz in group_devices]
    near_y = 1 - 2 * lax.rem(y, 2)
    plane_devices = [
        (xs[dx], lax.rem(y + 4 + near_y * dy, 4), cs[dc], z)
        for dx in (2, 1, 3, 0)
        for dy in (2, 3, 1, 0)
        for dc in range(2)
        if dx or dy > 1
    ]

    barrier = pltpu.get_barrier_semaphore()
    for device in group_devices + plane_devices:
        pl.semaphore_signal(barrier, inc=1, device_id=device, device_id_type=MESH)

    loads = []

    def load(src, dst):
        copy = pltpu.make_async_copy(src, dst, in_sem.at[len(loads)])
        copy.start()
        loads.append(copy)

    for src, dst in ((lw_hbm, lw_in), (lm_hbm, lm_in), (lv_hbm, lv_in), (lg_hbm, lg_in)):
        load(src, dst)
    slabs = [pl.multiple_of(up(inner + j, 7) * SUB, SUB) for j in range(4, 7)]
    local = pl.multiple_of(inner * SUB, SUB)
    pairs = ((w_hbm, w_in), (m_hbm, m_in), (v_hbm, v_in), (g_hbm, g_in))
    for src, dst in pairs:
        load(src.at[pl.ds(local, TILE), :], dst.at[pl.ds(local, TILE), :])
    for src, dst in pairs:
        for s in slabs:
            load(src.at[pl.ds(s, SUB), :], dst.at[pl.ds(s, SUB), :])

    load(owner_hbm, owner)

    steps = jnp.full((8, TILE), step_count[0], jnp.int32).astype(f32)
    num_scale = (LEARN_RATE / (1.0 - jnp.power(jnp.full((8, TILE), BETA_ONE, f32), steps)))[0:1]
    den_scale = (1.0 / (1.0 - jnp.power(jnp.full((8, TILE), BETA_TWO, f32), steps)))[0:1]

    for copy in loads[:4]:
        copy.wait()
    lat_rows = iota2((LROWS, TILE), 0)

    def lat_blocks(origin):
        start = (inner * 8 + origin) * LROWS
        return lax.div(start, TILE) * LBLOCKS, lat_rows < TILE - lax.rem(start, TILE)

    first_lane, in_first = lat_blocks(z)

    for b in range(LBLOCKS):
        cols = pl.ds(b * TILE, TILE)
        w1, m1, v1 = adamw(
            lw_in[:, cols], lm_in[:, cols], lv_in[:, cols], lg_in[:, cols], num_scale, den_scale
        )
        lw_out[:, cols] = w1
        lflat[b * LROWS : (b + 1) * LROWS, :] = w1
        lm_out[:, cols] = m1
        lv_out[:, cols] = v1
        size = jnp.abs(w1)
        lfold_a[b : b + 1, :] = jnp.max(
            jnp.where(in_first, size, 0.0), axis=0, keepdims=True
        )
        lfold_b[b : b + 1, :] = jnp.max(
            jnp.where(in_first, 0.0, size), axis=0, keepdims=True
        )
    real = iota2((16, 1), 0) < LBLOCKS
    max_a = jnp.where(real, jnp.max(lfold_a[...], axis=1, keepdims=True), 0.0)
    max_b = jnp.where(real, jnp.max(lfold_b[...], axis=1, keepdims=True), 0.0)
    lrow = jnp.maximum(lanes_of(max_a, first_lane), lanes_of(max_b, first_lane + LBLOCKS))
    lrow_out[0] = lrow
    lrow_in[place] = lrow

    def widest(fold):
        return jnp.max(jnp.max(fold[...], axis=1), axis=1, keepdims=True)

    loads[20].wait()

    @pl.loop(0, 16)
    def _(k):
        p = up(x + lax.div(k, 4), 4) * 4 + up(y + lax.rem(k, 4), 4)
        total = jnp.int32(0)
        for b in range(BLOCKS):
            total = jnp.maximum(total, jnp.where(owner[b] == p, b, 0))
        inverse[k] = total

    for copy in loads[4:8]:
        copy.wait()
    own = pl.ds(local, TILE)

    @pl.loop(0, BLOCKS)
    def _(b):
        cols = pl.ds(pl.multiple_of(b * TILE, TILE), TILE)
        w1, m1, v1 = adamw(
            w_in[own, cols], m_in[own, cols], v_in[own, cols], g_in[own, cols], num_scale, den_scale
        )
        w_out[own, cols] = w1
        w_blocks[b, own, :] = w1
        m_out[own, cols] = m1
        v_out[own, cols] = v1
        own_fold[b] = fold_rows(jnp.abs(w1))

    def spread(scale):
        return jnp.broadcast_to(scale, (16, TILE))

    def recip(scale):
        return spread(1.0 / (scale + SCALE_EPS))

    def put(ref, value):
        for b in range(BLOCKS):
            ref[b] = value[b : b + 1]

    own_max = widest(own_fold)
    put(own_scale, spread(own_max))
    put(own_recip, recip(own_max))

    def bulk_start(k, rows, count):
        pltpu.make_async_remote_copy(
            src_ref=send.at[k, pl.ds(rows, count), :],
            dst_ref=served.at[slot, pl.ds(rows, count), :],
            send_sem=bulk_send,
            recv_sem=bulk_recv,
            device_id=target(k),
            device_id_type=MESH,
        ).start()

    def bulk_home(rows, count):
        @pl.when(is_self)
        def _():
            served[slot, pl.ds(rows, count), :] = send[0, pl.ds(rows, count), :]

        @pl.when(jnp.logical_not(is_self))
        def _():
            bulk_start(0, rows, count)

    @pl.loop(0, 16)
    def _(k):
        b = inverse[k]
        send[k, own, :] = (w_blocks[b, own, :] * own_recip[b]).astype(bf16)

    pl.semaphore_wait(barrier, len(group_devices) + len(plane_devices))

    for device in group_devices:
        pltpu.make_async_remote_copy(
            src_ref=lrow_out.at[0],
            dst_ref=lrow_in.at[place],
            send_sem=lrow_send,
            recv_sem=lrow_recv,
            device_id=device,
            device_id_type=MESH,
        ).start()

    near = [
        pltpu.make_async_remote_copy(
            src_ref=lflat,
            dst_ref=lnear.at[way],
            send_sem=near_send.at[way],
            recv_sem=near_recv.at[way],
            device_id=(x, y, c, zs[step]),
            device_id_type=MESH,
        )
        for way, step in ((0, 1), (1, 7))
    ]
    for copy in near:
        copy.start()

    for k in SPREAD[:12]:
        bulk_start(k, local, TILE)

    for copy in loads[8:20]:
        copy.wait()

    @pl.loop(0, BLOCKS)
    def _(b):
        cols = pl.ds(pl.multiple_of(b * TILE, TILE), TILE)
        after = jnp.zeros((8, TILE), f32)
        before = jnp.zeros((8, TILE), f32)
        for j, s in zip(range(4, 7), slabs):
            rows = pl.ds(s, SUB)
            w1, m1, v1 = adamw(
                w_in[rows, cols], m_in[rows, cols], v_in[rows, cols], g_in[rows, cols],
                num_scale, den_scale,
            )
            w_out[rows, cols] = w1
            w_blocks[b, rows, :] = w1
            m_out[rows, cols] = m1
            v_out[rows, cols] = v1
            size = fold_rows(jnp.abs(w1))
            is_after = inner + j < 7
            after = jnp.maximum(after, jnp.where(is_after, size, 0.0))
            before = jnp.maximum(before, jnp.where(is_after, 0.0, size))
        next_fold[b] = after
        prev_fold[b] = before

    edge_out[0] = lanes_of(widest(next_fold), 0)
    edge_out[1] = lanes_of(widest(prev_fold), 0)

    def edge_copy(n, step):
        return pltpu.make_async_remote_copy(
            src_ref=edge_out.at[n],
            dst_ref=edge_in.at[n],
            send_sem=edge_send.at[n],
            recv_sem=edge_recv.at[n],
            device_id=(x, *quads[step], z),
            device_id_type=MESH,
        )

    edges = [edge_copy(0, 1), edge_copy(1, 3)]
    for copy in edges:
        copy.start()
    for k in SPREAD[12:]:
        bulk_start(k, local, TILE)
    bulk_home(local, TILE)

    for copy in edges:
        copy.wait_recv()
    prev_max = blocks_of(jnp.maximum(edge_out[1], edge_in[0]), 0)
    next_max = blocks_of(jnp.maximum(edge_out[0], edge_in[1]), 0)
    put(prev_recip, recip(prev_max))
    put(next_recip, recip(next_max))
    put(next_scale, spread(next_max))

    lane = iota2((1, TILE), 1)
    scale_lane = 7 * lax.div(slot, 4) + 2 * inner
    takes_next = jnp.logical_and(lane == scale_lane + 1, inner < 3)

    @pl.loop(0, 16)
    def _(k):
        b = inverse[k]
        value = jnp.where(lane == scale_lane, own_scale[b], 0.0)
        rows_out[k] = jnp.where(takes_next, next_scale[b], value)
        after = next_recip[b]
        before = prev_recip[b]
        for j, s in zip(range(4, 7), slabs):
            rows = pl.ds(s, SUB)
            scale = jnp.where(inner + j < 7, after, before)
            send[k, rows, :] = (w_blocks[b, rows, :] * scale).astype(bf16)

    def rows_start(k):
        pltpu.make_async_remote_copy(
            src_ref=rows_out.at[k],
            dst_ref=rows_all.at[slot],
            send_sem=rows_send,
            recv_sem=rows_recv,
            device_id=target(k),
            device_id_type=MESH,
        ).start()

    for k in range(1, 16):
        rows_start(k)

    @pl.when(is_self)
    def _():
        rows_all[slot] = rows_out[0]

    @pl.when(jnp.logical_not(is_self))
    def _():
        rows_start(0)

    few_rows = lrow_in.at[pl.ds(0, GROUP - 1)]
    pltpu.make_async_copy(few_rows, few_rows, lrow_recv).wait()
    lmax = jnp.max(lrow_in[...], axis=0)
    group = 2 * x + lax.div(y, 2)
    groups_out[0] = lmax
    groups_all[group] = lmax

    for dx, dy in [(dx, dy) for dx in range(4) for dy in (0, 2) if dx or dy]:
        pltpu.make_async_remote_copy(
            src_ref=groups_out.at[0],
            dst_ref=groups_all.at[group],
            send_sem=groups_send,
            recv_sem=groups_recv,
            device_id=(xs[dx], ys[dy], c, z),
            device_id_type=MESH,
        ).start()

    def shared_start(n):
        pieces = [(0, n * SUB), (n * SUB + TILE, ROWS - n * SUB - TILE)]

        @pl.when(inner == n)
        def _():
            for rows, count in pieces:
                if count:
                    for k in SPREAD:
                        bulk_start(k, rows, count)
                    bulk_home(rows, count)

    def lat_scale(src, origin):
        lane_a, in_a = lat_blocks(origin)
        scale_a = recip(blocks_of(lmax, lane_a))
        scale_b = recip(blocks_of(lmax, lane_a + LBLOCKS))
        for b in range(LBLOCKS):
            rows = slice(b * LROWS, (b + 1) * LROWS)
            scale = jnp.where(in_a, scale_a[b : b + 1, :], scale_b[b : b + 1, :])
            lscaled[rows, :] = src[rows, :] * scale
        lat[origin] = lscaled[...].astype(bf16)

    def ring_copy(way, hop, part):
        origin = up(z + 8 - hop, 8) if way == 0 else up(z + hop, 8)
        peer = up(z + 1, 8) if way == 0 else up(z + 7, 8)
        view = lat.at[origin, pl.ds(part * PART, PART), :]
        n = (way * 4 + hop) * PARTS + part
        return pltpu.make_async_remote_copy(
            src_ref=view,
            dst_ref=view,
            send_sem=ring_send.at[n],
            recv_sem=ring_recv.at[n],
            device_id=(x, y, c, peer),
            device_id_type=MESH,
        )

    def arrived(way, hop, part):
        origin = up(z + 7 - hop, 8) if way == 0 else up(z + 1 + hop, 8)
        view = lat.at[origin, pl.ds(part * PART, PART), :]
        n = (way * 4 + hop) * PARTS + part
        pltpu.make_async_copy(view, view, ring_recv.at[n]).wait()

    hops = [
        (way, hop, part)
        for hop in range(1, 4)
        for part in range(PARTS)
        for way in range(2)
        if hop < 3 or part == way
    ]
    sent = []

    def ring_start(way, hop, part):
        copy = ring_copy(way, hop, part)
        copy.start()
        sent.append(copy)

    for way, origin in ((0, up(z + 7, 8)), (1, up(z + 1, 8))):
        near[way].wait_recv()
        lat_scale(lnear.at[way], origin)
        for part in range(PARTS):
            ring_start(way, 1, part)

    for n in range(4):
        shared_start(n)
    lat_scale(lflat, z)

    for way, hop, part in hops:
        arrived(way, hop, part)
        if (way, hop + 1, part) in hops:
            ring_start(way, hop + 1, part)

    for copy in sent:
        copy.wait_send()
    for copy in edges:
        copy.wait_send()
    for copy in near:
        copy.wait_send()
    pltpu.make_async_copy(few_rows, few_rows, lrow_send).wait()
    seven = groups_all.at[pl.ds(0, 7)]
    pltpu.make_async_copy(seven, seven, groups_send).wait()
    pltpu.make_async_copy(seven, seven, groups_recv).wait()

    @pl.when(is_self)
    def _():
        rest = served.at[pl.ds(0, 15)]
        pltpu.make_async_copy(rest, rest, bulk_send).wait()
        pltpu.make_async_copy(rest, rest, bulk_recv).wait()
        rest = rows_all.at[pl.ds(0, 15)]
        pltpu.make_async_copy(rest, rest, rows_send).wait()
        pltpu.make_async_copy(rest, rest, rows_recv).wait()

    @pl.when(jnp.logical_not(is_self))
    def _():
        pltpu.make_async_copy(served, served, bulk_send).wait()
        pltpu.make_async_copy(served, served, bulk_recv).wait()
        pltpu.make_async_copy(rows_all, rows_all, rows_send).wait()
        pltpu.make_async_copy(rows_all, rows_all, rows_recv).wait()


def store_kernel(
    w_in,
    m_in,
    v_in,
    served_in,
    rows_in,
    groups_in,
    lw_in,
    lm_in,
    lv_in,
    lat_in,
    w_hbm,
    m_hbm,
    v_hbm,
    served_hbm,
    scales_hbm,
    lw_hbm,
    lm_hbm,
    lv_hbm,
    lserved_hbm,
    lscales_hbm,
    lserved,
    ltall,
    lflat,
    scales,
    lscales,
    lscales_tall,
    sem,
):
    copies = []

    def store(src, dst):
        copy = pltpu.make_async_copy(src, dst, sem.at[len(copies)])
        copy.start()
        copies.append(copy)

    for src, dst in (
        (w_in, w_hbm),
        (m_in, m_hbm),
        (v_in, v_hbm),
        (served_in, served_hbm),
        (lw_in, lw_hbm),
        (lm_in, lm_hbm),
        (lv_in, lv_hbm),
    ):
        store(src, dst)
    for o in range(8):
        lflat[...] = lat_in[o].astype(f32)
        for b in range(LBLOCKS):
            ltall[o * LROWS : (o + 1) * LROWS, b * TILE : (b + 1) * TILE] = lflat[
                b * LROWS : (b + 1) * LROWS, :
            ]
    lserved[...] = ltall[...].astype(bf16)
    store(lserved, lserved_hbm)
    scales[...] = jnp.max(rows_in[...], axis=0)[:, 0:28]
    for g in range(8):
        group = groups_in[g]
        for r in range(7):
            lane = r * LBLOCKS
            lscales_tall[7 * g + r : 7 * g + r + 1, 0:LBLOCKS] = group[:, lane : lane + LBLOCKS]
    lscales[...] = lscales_tall[...].T[0:LBLOCKS, 0:56]
    store(scales, scales_hbm)
    store(lscales, lscales_hbm)
    for copy in copies:
        copy.wait()


def body(
    expert_master,
    expert_first,
    expert_second,
    expert_grad,
    latent_master,
    latent_first,
    latent_second,
    latent_grad,
    step_count,
    column_owner,
):
    hbm = pl.BlockSpec(memory_space=pltpu.HBM)
    vmem = pl.BlockSpec(memory_space=pltpu.VMEM)
    dma = pltpu.SemaphoreType.DMA
    row = (1, TILE)
    made = pl.pallas_call(
        step_kernel,
        out_shape=(
            pltpu.VMEM((ROWS, COLS), f32),
            pltpu.VMEM((ROWS, COLS), bf16),
            pltpu.VMEM((ROWS, COLS), bf16),
            pltpu.VMEM((16, ROWS, TILE), bf16),
            pltpu.VMEM((16, *row), f32),
            pltpu.VMEM((8, *row), f32),
            pltpu.VMEM((LROWS, LCOLS), f32),
            pltpu.VMEM((LROWS, LCOLS), bf16),
            pltpu.VMEM((LROWS, LCOLS), bf16),
            pltpu.VMEM((8, LFLAT, TILE), bf16),
        ),
        in_specs=[pl.BlockSpec(memory_space=pltpu.SMEM)] + [hbm] * 9,
        out_specs=(vmem,) * 10,
        scratch_shapes=[
            pltpu.VMEM((ROWS, COLS), f32),
            pltpu.VMEM((ROWS, COLS), bf16),
            pltpu.VMEM((ROWS, COLS), bf16),
            pltpu.VMEM((ROWS, COLS), bf16),
            pltpu.VMEM((LROWS, LCOLS), f32),
            pltpu.VMEM((LROWS, LCOLS), bf16),
            pltpu.VMEM((LROWS, LCOLS), bf16),
            pltpu.VMEM((LROWS, LCOLS), bf16),
            pltpu.VMEM((16, ROWS, TILE), f32),
            pltpu.VMEM((16, ROWS, TILE), bf16),
            pltpu.VMEM((16, 8, TILE), f32),
            pltpu.VMEM((16, 8, TILE), f32),
            pltpu.VMEM((16, 8, TILE), f32),
            pltpu.VMEM((16, *row), f32),
            pltpu.VMEM((16, *row), f32),
            pltpu.VMEM((16, *row), f32),
            pltpu.VMEM((16, *row), f32),
            pltpu.VMEM((16, *row), f32),
            pltpu.VMEM((16, TILE), f32),
            pltpu.VMEM((16, TILE), f32),
            pltpu.VMEM((1, *row), f32),
            pltpu.VMEM((GROUP, *row), f32),
            pltpu.VMEM((2, *row), f32),
            pltpu.VMEM((2, *row), f32),
            pltpu.VMEM((16, *row), f32),
            pltpu.VMEM((1, *row), f32),
            pltpu.VMEM((LFLAT, TILE), f32),
            pltpu.VMEM((LFLAT, TILE), f32),
            pltpu.VMEM((2, LFLAT, TILE), f32),
            pltpu.SMEM((16,), jnp.int32),
            pltpu.SMEM((16,), jnp.int32),
            dma((21,)),
            dma,
            dma,
            dma,
            dma,
            dma((2,)),
            dma((2,)),
            dma((2,)),
            dma((2,)),
            dma,
            dma,
            dma,
            dma,
            dma((8 * PARTS,)),
            dma((8 * PARTS,)),
        ],
        compiler_params=pltpu.CompilerParams(
            collective_id=0, has_side_effects=True, vmem_limit_bytes=24 << 20
        ),
        name="step",
    )(
        pltpu.with_memory_space_constraint(step_count, pltpu.SMEM),
        *(
            pltpu.with_memory_space_constraint(value, pltpu.HBM)
            for value in (
                column_owner,
                expert_master[0],
                expert_first[0],
                expert_second[0],
                expert_grad[0],
                latent_master,
                latent_first,
                latent_second,
                latent_grad,
            )
        ),
    )
    out = pl.pallas_call(
        store_kernel,
        out_shape=(
            jax.ShapeDtypeStruct((ROWS, COLS), f32),
            jax.ShapeDtypeStruct((ROWS, COLS), bf16),
            jax.ShapeDtypeStruct((ROWS, COLS), bf16),
            jax.ShapeDtypeStruct((16, ROWS, TILE), bf16),
            jax.ShapeDtypeStruct((1, 28), f32),
            jax.ShapeDtypeStruct((LROWS, LCOLS), f32),
            jax.ShapeDtypeStruct((LROWS, LCOLS), bf16),
            jax.ShapeDtypeStruct((LROWS, LCOLS), bf16),
            jax.ShapeDtypeStruct((ROWS, LCOLS), bf16),
            jax.ShapeDtypeStruct((LBLOCKS, 56), f32),
        ),
        in_specs=[vmem] * 10,
        out_specs=(hbm,) * 10,
        scratch_shapes=[
            pltpu.VMEM((ROWS, LCOLS), bf16),
            pltpu.VMEM((ROWS, LCOLS), f32),
            pltpu.VMEM((LFLAT, TILE), f32),
            pltpu.VMEM((1, 28), f32),
            pltpu.VMEM((LBLOCKS, 56), f32),
            pltpu.VMEM((TILE, TILE), f32),
            dma((10,)),
        ],
        compiler_params=pltpu.CompilerParams(vmem_limit_bytes=8 << 20),
        name="store",
    )(*made)
    master, first, second, served, scales, lmaster, lfirst, lsecond, lserved, lscales = out
    return (
        master[None],
        first[None],
        second[None],
        served.reshape(1, 16 * ROWS, TILE),
        scales,
        lmaster,
        lfirst,
        lsecond,
        lserved,
        lscales.T,
    )


def solution(mesh):
    torus = Mesh(
        mesh.devices.reshape(4, 4, 2, mesh.shape["expert"]), ("dp_0", "dp_1", "dp_2", "expert")
    )
    expert = P("expert", DP, None)
    latent = P(DP_EXPERT, None)
    return jax.shard_map(
        body,
        mesh=torus,
        in_specs=(expert,) * 4 + (latent,) * 4 + (P(), P()),
        out_specs=(
            expert,
            expert,
            expert,
            expert,
            P("expert", DP),
            latent,
            latent,
            latent,
            P(DP, None),
            P(),
        ),
        check_vma=False,
    )
```
